32 devices in a mesh: seq: 2 (over x), fsdp: 16 (over z, y, core).
Axes of the slice: x: 2, y: 2, z: 4, core: 2. Of those that a mesh axis runs over, the one named last changes fastest.
Arguments:
- tokens: bfloat16 [6656, 1536], P(('fsdp', 'seq')), may hold values from -6 to 6
- conditioning: bfloat16 [2048, 1536], P('fsdp'), may hold values from -6 to 6
- seq_lengths: int32 [16], replicated, may hold values from 52 to 416, as said below
- cond_lengths: int32 [16], replicated, may hold values from 32 to 128, as said below
- norm_gains: bfloat16 [3, 1536], P(None, ('seq', 'fsdp')), may hold values from 0.25 to 1.75
- w_qkv: bfloat16 [1536, 4608], P(('seq', 'fsdp')), may hold values from -0.21875 to 0.21875
- w_self_out: bfloat16 [1536, 1536], P(('seq', 'fsdp')), may hold values from -0.4375 to 0.4375
- w_cross_q: bfloat16 [1536, 1536], P(('seq', 'fsdp')), may hold values from -0.15625 to 0.15625
- w_cross_kv: bfloat16 [1536, 3072], P(('seq', 'fsdp')), may hold values from -0.15625 to 0.15625
- w_cross_out: bfloat16 [1536, 1536], P(('seq', 'fsdp')), may hold values from -0.875 to 0.875
- w_gate_up: bfloat16 [1536, 12288], P(('seq', 'fsdp')), may hold values from -0.15625 to 0.15625
- w_down: bfloat16 [6144, 1536], P(('seq', 'fsdp')), may hold values from -0.15625 to 0.15625
- out_grad: bfloat16 [6656, 1536], P(('fsdp', 'seq')), may hold values from -6 to 6
Outputs:
- block_out: bfloat16 [6656, 1536], P(('fsdp', 'seq'))
- d_tokens: float32 [6656, 1536], P(('fsdp', 'seq'))
- d_conditioning: float32 [2048, 1536], P('fsdp')
- d_norm_gains: float32 [3, 1536], P(None, ('seq', 'fsdp'))
- d_w_qkv: float32 [1536, 4608], P(('seq', 'fsdp'))
- d_w_self_out: float32 [1536, 1536], P(('seq', 'fsdp'))
- d_w_cross_q: float32 [1536, 1536], P(('seq', 'fsdp'))
- d_w_cross_kv: float32 [1536, 3072], P(('seq', 'fsdp'))
- d_w_cross_out: float32 [1536, 1536], P(('seq', 'fsdp'))
- d_w_gate_up: float32 [1536, 12288], P(('seq', 'fsdp'))
- d_w_down: float32 [6144, 1536], P(('seq', 'fsdp'))
- rms_stats: float32 [6], replicated
The draws below stay inside these ranges and needn't reach their ends.
Inputs may be any that keep to these rules, and one draw needn't show every extreme that they name: A sequence's valid latent tokens are its first seq_lengths positions; in every draw some sequence has all 416 valid. A sequence's valid conditioning tokens are its first cond_lengths ones; in every draw some sequence has all 128 valid.
All inputs are finite; a program needn't handle non-finite values.
Results may differ from the reference program's by a relative error of at most 0.024.
Values may be sent and summed in bfloat16 or wider, within the bound.
No kernel may reach another device: no remote copies, remote signals or barrier semaphores. Data moves between devices by JAX's collectives and lax.ppermute only.
A program may use at most 768 MiB of HBM per device.

```python
import math
import jax
import jax.numpy as jnp
from jax import lax

D = 1536
HEADS = 24
HD = 64
FF = 6144
CT = 128
LEN = 416
SEQS = 16
TOKENS = 6656


def draw_seq_lengths(key, part):
    base_values = jax.random.randint(jax.random.fold_in(key, 11), (SEQS,), LEN // 8, LEN + 1)
    full_index = jax.random.randint(jax.random.fold_in(key, 12), (), 0, SEQS)
    return jnp.where(jnp.arange(SEQS) == full_index, LEN, base_values).astype(jnp.int32)


def draw_cond_lengths(key, part):
    base_values = jax.random.randint(jax.random.fold_in(key, 21), (SEQS,), CT // 4, CT + 1)
    full_index = jax.random.randint(jax.random.fold_in(key, 22), (), 0, SEQS)
    return jnp.where(jnp.arange(SEQS) == full_index, CT, base_values).astype(jnp.int32)


def block_scale(stream_key, extent, cuts, low, high):
    def one(dim, parts):
        draws = jax.random.uniform(jax.random.fold_in(jax.random.fold_in(stream_key, 6), dim), (parts,), jnp.float32, low / len(cuts), high / len(cuts))
        return jnp.repeat(jnp.exp(draws), extent[dim] // parts).reshape((-1,) + (1,) * (len(extent) - dim - 1))

    loudness = one(*cuts[0])
    for cut in cuts[1:]:
        loudness = loudness * one(*cut)
    return loudness


def noise(own_key, extent, deviation, bound, split=(), kind=jnp.bfloat16):
    loudness = block_scale(own_key, extent, split, -0.22, 0.18) if split else 1.0
    drawn = jax.random.normal(own_key, extent, jnp.float32) * deviation * loudness
    return jnp.minimum(jnp.maximum(drawn, -bound), bound).astype(kind)


def setup_inputs(seed: int = 0) -> dict:
    streams_of = jax.random.split(jax.random.key(seed), 14)
    tokens = noise(streams_of[0], (TOKENS, D), 1.0, 6.0, ((0, 32),))
    conditioning = noise(streams_of[1], (SEQS * CT, D), 1.0, 6.0, ((0, 16),))
    seq_lengths = draw_seq_lengths(jax.random.fold_in(streams_of[13], 71), 0)
    cond_lengths = draw_cond_lengths(jax.random.fold_in(streams_of[13], 71), 0)
    norm_gains = jnp.clip(1.0 + 0.15 * jax.random.normal(streams_of[4], (3, D), jnp.float32), 0.25, 1.75).astype(jnp.bfloat16)
    w_qkv = noise(streams_of[5], (D, 3 * D), (D // 2) ** -0.5, 0.21875, ((0, 32),))
    w_self_out = noise(streams_of[6], (D, D), (D // 8) ** -0.5, 0.4375, ((0, 32),))
    w_cross_q = noise(streams_of[7], (D, D), D ** -0.5, 0.15625, ((0, 32),))
    w_cross_kv = noise(streams_of[8], (D, 2 * D), D ** -0.5, 0.15625, ((0, 32),))
    w_cross_out = noise(streams_of[9], (D, D), (D // 32) ** -0.5, 0.875, ((0, 32),))
    w_gate_up = noise(streams_of[10], (D, 2 * FF), D ** -0.5, 0.15625, ((0, 32),))
    w_down = noise(streams_of[11], (FF, D), (FF // 4) ** -0.5, 0.15625, ((0, 32),))
    out_grad = noise(streams_of[12], (TOKENS, D), 1.0, 6.0, ((0, 32),))
    return {"tokens": tokens, "conditioning": conditioning, "seq_lengths": seq_lengths, "cond_lengths": cond_lengths, "norm_gains": norm_gains, "w_qkv": w_qkv, "w_self_out": w_self_out, "w_cross_q": w_cross_q, "w_cross_kv": w_cross_kv, "w_cross_out": w_cross_out, "w_gate_up": w_gate_up, "w_down": w_down, "out_grad": out_grad}


@jax.custom_vjp
def low(v):
    return lax.optimization_barrier(v.astype(jnp.bfloat16)).astype(jnp.float32)

@jax.custom_vjp
def low_back(v):
    return v

def low_keep(v):
    return (low(v), None)

def low_pass(kept, grad):
    return (grad,)

def back_keep(v):
    return (v, None)

def back_low(kept, grad):
    return (low(grad),)
low.defvjp(low_keep, low_pass)
low_back.defvjp(back_keep, back_low)

def matmul_high(left_side, right_side):
    return jnp.dot(left_side, right_side, precision=lax.Precision.HIGHEST, preferred_element_type=jnp.float32)

def layer_norm(hidden_rows, gain_row):
    centred = hidden_rows - lax.optimization_barrier(jnp.mean(hidden_rows, axis=-1, keepdims=True))
    variance = lax.optimization_barrier(jnp.mean(centred * centred, axis=-1, keepdims=True))
    return centred * lax.rsqrt(variance + 1e-05) * gain_row

def rope_tables(positions):
    freqs = jnp.exp(jnp.arange(16, dtype=jnp.float32) * (-math.log(10000.0) / 16.0))
    angles = positions[:, None] * freqs[None, :]
    return (jnp.cos(angles)[:, None, :], jnp.sin(angles)[:, None, :])

def rotate(values, cosine, sine):
    first_part = values[..., :16]
    second_part = values[..., 16:32]
    return jnp.concatenate([first_part * cosine - second_part * sine, second_part * cosine + first_part * sine, values[..., 32:]], axis=-1)

def attend_block(query, keys, values, valid):
    scores = low_back(jnp.einsum('qhd,khd->hqk', query, keys, precision=lax.Precision.HIGHEST) * 0.125)
    scores = jnp.where(valid[None, None, :], scores, -1e+30)
    peak = lax.optimization_barrier(jnp.max(scores, axis=-1, keepdims=True))
    expo = jnp.exp(scores - peak)
    probs = low(expo / lax.optimization_barrier(jnp.sum(expo, axis=-1, keepdims=True)))
    return jnp.einsum('hqk,khd->qhd', probs, values, precision=lax.Precision.HIGHEST)

def attention(query, keys, values, valid):
    seq_length = query.shape[1]
    block_count = max(1, seq_length // 512)
    block_fn = jax.checkpoint(attend_block)

    def one_sequence(query_seq, keys_seq, values_seq, valid_seq):
        blocks = query_seq.reshape(block_count, seq_length // block_count, query_seq.shape[1], query_seq.shape[2])
        mixed = lax.map(lambda block_rows: block_fn(block_rows, keys_seq, values_seq, valid_seq), blocks)
        return mixed.reshape(query_seq.shape)
    seq_fn = jax.checkpoint(one_sequence)
    return lax.map(lambda entry_data: seq_fn(entry_data[0], entry_data[1], entry_data[2], entry_data[3]), (query, keys, values, valid))

def reference(tokens, conditioning, seq_lengths, cond_lengths, norm_gains, w_qkv, w_self_out, w_cross_q, w_cross_kv, w_cross_out, w_gate_up, w_down, out_grad):
    total_rows = SEQS * LEN
    valid_count = jnp.sum(seq_lengths).astype(jnp.float32)
    row_valid = (jnp.arange(LEN, dtype=jnp.int32)[None, :] < seq_lengths[:, None]).reshape(total_rows).astype(jnp.float32)
    key_valid = jnp.arange(LEN, dtype=jnp.int32)[None, :] < seq_lengths[:, None]
    cond_valid = jnp.arange(CT, dtype=jnp.int32)[None, :] < cond_lengths[:, None]
    cosine, sine = rope_tables(jnp.arange(LEN).astype(jnp.float32))

    def mean_square(rows_value):
        return jnp.sqrt(jnp.sum(rows_value * rows_value * row_valid[:, None]) / (valid_count * D))

    def forward(x_rows, cond_rows, gains, qkv_weight, self_out_weight, cross_q_weight, cross_kv_weight, cross_out_weight, gate_up_weight, down_weight):
        norm_first = low(layer_norm(x_rows, gains[0]))
        projected = matmul_high(norm_first, qkv_weight)
        query = low(rotate(low_back(projected[:, :D]).reshape(SEQS, LEN, HEADS, HD), cosine, sine))
        keys = low(rotate(low_back(projected[:, D:2 * D]).reshape(SEQS, LEN, HEADS, HD), cosine, sine))
        values = low(low_back(projected[:, 2 * D:])).reshape(SEQS, LEN, HEADS, HD)
        self_mixed = attention(query, keys, values, key_valid)
        self_mixed = low(low_back(self_mixed.reshape(total_rows, D)))
        self_branch = low_back(matmul_high(self_mixed, self_out_weight))
        after_self = x_rows + self_branch
        norm_second = low(layer_norm(after_self, gains[1]))
        cross_query = low(low_back(matmul_high(norm_second, cross_q_weight))).reshape(SEQS, LEN, HEADS, HD)
        cond_proj = low(low_back(matmul_high(cond_rows, cross_kv_weight)))
        cond_keys = cond_proj[:, :D].reshape(SEQS, CT, HEADS, HD)
        cond_values = cond_proj[:, D:].reshape(SEQS, CT, HEADS, HD)
        cross_mixed = attention(cross_query, cond_keys, cond_values, cond_valid)
        cross_mixed = low(low_back(cross_mixed.reshape(total_rows, D)))
        cross_branch = low_back(matmul_high(cross_mixed, cross_out_weight))
        after_cross = after_self + cross_branch
        norm_third = low(layer_norm(after_cross, gains[2]))
        gate_up = low_back(matmul_high(norm_third, gate_up_weight))
        hidden = low(jax.nn.silu(gate_up[:, :FF]) * gate_up[:, FF:])
        mlp_branch = low_back(matmul_high(hidden, down_weight))
        block_sum = after_cross + mlp_branch
        stats = jnp.stack([mean_square(self_branch), mean_square(after_self), mean_square(cross_branch), mean_square(after_cross), mean_square(mlp_branch), mean_square(block_sum)])
        return (block_sum, stats)
    block_sum, pull_back, stats = jax.vjp(forward, tokens.astype(jnp.float32), conditioning.astype(jnp.float32), norm_gains.astype(jnp.float32), w_qkv.astype(jnp.float32), w_self_out.astype(jnp.float32), w_cross_q.astype(jnp.float32), w_cross_kv.astype(jnp.float32), w_cross_out.astype(jnp.float32), w_gate_up.astype(jnp.float32), w_down.astype(jnp.float32), has_aux=True)
    grads = pull_back(out_grad.astype(jnp.float32))
    return (block_sum.astype(jnp.bfloat16), grads[0], grads[1], grads[2], grads[3], grads[4], grads[5], grads[6], grads[7], grads[8], grads[9], stats)
```

```python
import functools
import math

import jax
import jax.numpy as jnp
from jax import lax
from jax.experimental import pallas as pl
from jax.experimental.pallas import tpu as pltpu
from jax.sharding import Mesh, PartitionSpec as P

HD = 64
LANES = 128
BF = jnp.bfloat16
F32 = jnp.float32
ALL = ("s", "z", "y", "c")


def swap(value, axis):
    return lax.ppermute(value, axis, [(0, 1), (1, 0)])


def gather_four(own):
    across_s = swap(own, "s")
    return jnp.concatenate([own, across_s, swap(own, "c"), swap(across_s, "c")], axis=0)


def reduce_four(partial, rows):
    parts = partial.reshape(2, 2, rows, partial.shape[-1])
    merged = parts[0] + swap(parts[1].astype(BF), "c").astype(F32)
    return merged[0] + swap(merged[1].astype(BF), "s").astype(F32)


def gather_eight(own):
    half = own.shape[0] // 2
    across_s = swap(own, "s")
    across_y = swap(own, "y")
    far_low = swap(across_y[:half], "s")
    far_high = swap(across_s[half:], "y")
    chip = [own, across_s, across_y, far_low, far_high]
    return jnp.concatenate(chip + [swap(block, "c") for block in chip], axis=0)


def reduce_eight(partial, rows):
    width = partial.shape[-1]
    half = rows // 2
    parts = partial.reshape(2, 4, rows, width)
    merged = parts[0] + swap(parts[1].astype(BF), "c").astype(F32)
    low, high = merged[:, :half], merged[:, half:]
    low_got = swap(jnp.stack([low[1], low[3]]).astype(BF), "s").astype(F32)
    high_got = swap(jnp.stack([high[2], high[3]]).astype(BF), "y").astype(F32)
    low_own, low_y = low[0] + low_got[0], low[2] + low_got[1]
    high_own, high_s = high[0] + high_got[0], high[1] + high_got[1]
    low_sum = low_own + swap(low_y.astype(BF), "y").astype(F32)
    high_sum = high_own + swap(high_s.astype(BF), "s").astype(F32)
    return jnp.concatenate([low_sum, high_sum], axis=0)


def gather_z(value):
    return lax.all_gather(value, "z", axis=0, tiled=True)


def scatter_z(value):
    return lax.psum_scatter(value, "z", scatter_dimension=0, tiled=True)


def after(value, earlier):
    return lax.optimization_barrier((value, earlier))[0]


def spread_columns(weight, blocks, gain, group):
    rows = gain.shape[0]
    scaled = (weight.astype(F32) * gain[:, None]).astype(BF)
    parts = jnp.moveaxis(scaled.reshape(rows, blocks, 4, -1), 2, 0).reshape(4, rows, -1)
    return lax.all_to_all(parts, group, 0, 0, tiled=True)


def attention_rows(column, rows):
    width = column.shape[1]
    own = column.reshape(-1, 2, 2 * rows, width)
    other = swap(own, "y")
    first = lax.axis_index("y") == 0
    both = jnp.stack([jnp.where(first, own, other), jnp.where(first, other, own)], axis=2)
    return jnp.moveaxis(both, 0, 1).reshape(-1, width)


def attention_rows_back(grad, group):
    width = grad.shape[1]
    z_count = lax.axis_size("z")
    rows = grad.shape[0] // (8 * z_count)
    y_rank = lax.axis_index("y")
    view = grad.reshape(2, z_count, 2, 2 * rows, width)
    mine = lax.dynamic_index_in_dim(view, y_rank, 2, keepdims=False)
    theirs = lax.dynamic_index_in_dim(view, 1 - y_rank, 2, keepdims=False)
    total = mine + swap(theirs.astype(BF), "y").astype(F32)
    total = jnp.moveaxis(total, 0, 1).astype(BF).reshape(-1, width)
    owned = scatter_z(total).reshape(4, rows, width)
    got = lax.all_to_all(owned, group, 0, 0, tiled=True)
    got = got.reshape(4, rows, 3, width // 3)
    return jnp.moveaxis(got, 0, 2).reshape(rows, 3, -1).astype(F32)


def head_rows(column, rows):
    width = column.shape[-1]
    half = lax.axis_size("z") // 2
    mine = lax.all_to_all(column.reshape(2, half, rows, width), "c", 0, 0, tiled=True)
    other = swap(mine, "y")
    first = lax.axis_index("y") == 0
    both = jnp.stack([jnp.where(first, mine, other), jnp.where(first, other, mine)])
    return jnp.transpose(both, (2, 0, 1, 3, 4)).reshape(-1, width)


def head_rows_back(grad):
    z_count = lax.axis_size("z")
    width = grad.shape[1]
    half = z_count // 2
    rows = grad.shape[0] // (4 * half)
    y_rank = lax.axis_index("y")
    view = grad.reshape(half, 2, 2, rows, width)
    mine = lax.dynamic_index_in_dim(view, y_rank, 1, keepdims=False)
    theirs = lax.dynamic_index_in_dim(view, 1 - y_rank, 1, keepdims=False)
    total = mine + swap(theirs.astype(BF), "y").astype(F32)
    total = jnp.moveaxis(total, 1, 0).astype(BF)
    column = lax.all_to_all(total, "c", 0, 0, tiled=True).reshape(z_count * rows, width)
    return scatter_z(column).astype(F32)


def gained(grad, weight, gain):
    return grad * gain[:, None], jnp.sum(grad * weight.astype(F32), axis=1)


def head_masks(shape):
    lane = lax.broadcasted_iota(jnp.int32, shape, 1)
    return lane < HD


def rotate(values, cos_ref, down_ref, up_ref, sign):
    ahead = pltpu.roll(values, LANES - 16, 1)
    behind = pltpu.roll(values, 16, 1)
    return values * cos_ref[...] + sign * (ahead * down_ref[...] + behind * up_ref[...])


def nt(left, right):
    return lax.dot_general(left, right, (((1,), (1,)), ((), ())), preferred_element_type=F32)


def tn(left, right):
    return lax.dot_general(left, right, (((0,), (0,)), ((), ())), preferred_element_type=F32)


def nn(left, right):
    return lax.dot_general(left, right, (((1,), (0,)), ((), ())), preferred_element_type=F32)


def forward_heads(query, keys, values, valid):
    left = head_masks(query.shape)
    outs, logs = [], []
    for head in range(2):
        picked = left if head == 0 else jnp.logical_not(left)
        scores = nt(jnp.where(picked, query, jnp.zeros_like(query)), keys) * 0.125
        scores = jnp.where(valid, scores, -1e30)
        peak = jnp.max(scores, axis=-1, keepdims=True)
        expo = jnp.exp(scores - peak)
        total = jnp.sum(expo, axis=-1, keepdims=True)
        probs = (expo * (1.0 / total)).astype(BF)
        outs.append(nn(probs, values))
        logs.append(peak + jnp.log(total))
    return (
        jnp.where(left, outs[0], outs[1]).astype(BF),
        jnp.where(left, logs[0], logs[1]),
    )


def backward_heads(query, keys, values, valid, logsum, grad):
    left = head_masks(query.shape)
    left_keys = head_masks(keys.shape)
    grad_q, grad_k, grad_v = [], [], []
    for head in range(2):
        picked = left if head == 0 else jnp.logical_not(left)
        none = jnp.zeros_like(query)
        scores = nt(jnp.where(picked, query, none), keys) * 0.125
        scores = jnp.where(valid, scores, -1e30)
        probs = jnp.exp(scores - logsum[:, head * HD : head * HD + 1])
        grad_probs = nt(jnp.where(picked, grad, none), values)
        delta = jnp.sum(probs * grad_probs, axis=-1, keepdims=True)
        grad_scores = (probs * (grad_probs - delta)).astype(BF)
        grad_q.append(nn(grad_scores, keys))
        grad_k.append(tn(grad_scores, query))
        grad_v.append(tn(probs.astype(BF), grad))
    return (
        jnp.where(left, grad_q[0], grad_q[1]) * 0.125,
        jnp.where(left_keys, grad_k[0], grad_k[1]) * 0.125,
        jnp.where(left_keys, grad_v[0], grad_v[1]),
    )


def self_forward_kernel(
    lengths, position, cosine, down, up, query, keys, values, query_out, keys_out, values_out, mixed, logsum
):
    query_rot = rotate(query[...], cosine, down, up, 1.0).astype(BF)
    keys_rot = rotate(keys[...], cosine, down, up, 1.0).astype(BF)
    values_low = values[...].astype(BF)
    query_out[...] = query_rot
    keys_out[...] = keys_rot
    values_out[...] = values_low
    valid = position[0:1, :] < lengths[pl.program_id(0)]
    mixed[...], logsum[...] = forward_heads(query_rot, keys_rot, values_low, valid)


def self_backward_kernel(
    lengths, position, cosine, down, up, query, keys, values, logsum, grad, grad_q, grad_k, grad_v
):
    valid = position[0:1, :] < lengths[pl.program_id(0)]
    back_q, back_k, back_v = backward_heads(
        query[...], keys[...], values[...], valid, logsum[...], grad[...]
    )
    grad_q[...] = rotate(back_q, cosine, down, up, -1.0).astype(BF)
    grad_k[...] = rotate(back_k, cosine, down, up, -1.0).astype(BF)
    grad_v[...] = back_v.astype(BF)


def cross_forward_kernel(lengths, position, query, keys, values, mixed, logsum):
    valid = position[0:1, :] < lengths[pl.program_id(0)]
    mixed[...], logsum[...] = forward_heads(query[...], keys[...], values[...], valid)


def cross_backward_kernel(
    lengths, position, query, keys, values, logsum, grad, grad_q, grad_k, grad_v
):
    valid = position[0:1, :] < lengths[pl.program_id(0)]
    back_q, back_k, back_v = backward_heads(
        query[...], keys[...], values[...], valid, logsum[...], grad[...]
    )
    grad_q[...] = back_q.astype(BF)
    grad_k[...] = back_k.astype(BF)
    grad_v[...] = back_v.astype(BF)


def attention_call(kernel, lengths, tables, pairs, inputs, outputs, name):
    sequences = lengths.shape[0]

    def block(rows, first):
        return pl.BlockSpec((rows, LANES), lambda b, j, ln, first=first: (b, first + j))

    def whole(table):
        return pl.BlockSpec(table.shape, lambda b, j, ln: (0, 0))

    flops = 0
    return pl.pallas_call(
        kernel,
        out_shape=[jax.ShapeDtypeStruct((sequences * rows, pairs * LANES), dt) for rows, dt in outputs],
        grid_spec=pltpu.PrefetchScalarGridSpec(
            num_scalar_prefetch=1,
            grid=(sequences, pairs),
            in_specs=[whole(t) for t in tables] + [block(r, f) for _, r, f in inputs],
            out_specs=[block(r, 0) for r, _ in outputs],
        ),
        compiler_params=pltpu.CompilerParams(
            dimension_semantics=("arbitrary", "arbitrary"), vmem_limit_bytes=48 << 20
        ),
        name=name,
    )(lengths, *tables, *[a for a, _, _ in inputs])


def normalize(hidden):
    centred = hidden - jnp.mean(hidden, axis=-1, keepdims=True)
    inverse = lax.rsqrt(jnp.mean(centred * centred, axis=-1, keepdims=True) + 1e-05)
    return centred * inverse, inverse


def layer_norm(hidden):
    return normalize(hidden)[0].astype(BF)


def layer_norm_back(hidden, scaled):
    unit, inverse = normalize(hidden)
    return inverse * (
        scaled
        - jnp.mean(scaled, axis=-1, keepdims=True)
        - unit * jnp.mean(scaled * unit, axis=-1, keepdims=True)
    )


def masked_square(rows_value, row_weight):
    return jnp.sum(rows_value * rows_value * row_weight[:, None])


def shards(
    tokens,
    conditioning,
    seq_lengths,
    cond_lengths,
    norm_gains,
    w_qkv,
    w_self_out,
    w_cross_q,
    w_cross_kv,
    w_cross_out,
    w_gate_up,
    w_down,
    out_grad,
):
    rows, width = tokens.shape
    z_count = lax.axis_size("z")
    own_rows = w_qkv.shape[0]
    hidden_own = w_down.shape[0]
    s_rank, z_rank = lax.axis_index("s"), lax.axis_index("z")
    y_rank, c_rank = lax.axis_index("y"), lax.axis_index("c")
    part = width // 4
    pairs = part // LANES
    span = 2 * rows

    first_seq = (z_rank * 2 + y_rank) * 2
    mine, other = first_seq + c_rank, first_seq + 1 - c_rank
    seq_two = jnp.stack([seq_lengths[mine], seq_lengths[other]])
    cond_two = jnp.stack([cond_lengths[mine], cond_lengths[other]])
    steps = jnp.arange(rows, dtype=jnp.int32)
    positions = jnp.concatenate([s_rank * rows + steps, (1 - s_rank) * rows + steps])
    row_valid = (positions[:rows] < seq_two[0]).astype(F32)
    lane = jnp.arange(LANES, dtype=jnp.int32) % HD
    freqs = jnp.exp((lane % 16).astype(F32) * (-math.log(10000.0) / 16.0))
    angles = positions.astype(F32)[:, None] * freqs[None, :]
    cosine = jnp.where(lane < 32, jnp.cos(angles), 1.0)
    sine = jnp.sin(angles)
    down = jnp.where(lane < 16, -sine, 0.0)
    up = jnp.where((lane >= 16) & (lane < 32), sine, 0.0)
    key_position = jnp.broadcast_to(positions[None, :], (8, span))
    cond_rows = conditioning.shape[0]
    cond_position = jnp.broadcast_to(jnp.arange(cond_rows, dtype=jnp.int32)[None, :], (8, cond_rows))

    four, eight = ("s", "c"), ("s", "y", "c")
    gains = norm_gains.astype(F32)
    qkv_parts = spread_columns(w_qkv, 3, gains[0], four)
    cross_weights = after((w_cross_q, w_cross_kv), qkv_parts)
    qkv_column = gather_z(qkv_parts.reshape(4 * own_rows, -1))
    outs_column = gather_z(after(jnp.concatenate([w_self_out, w_cross_out], axis=0), qkv_column))
    cross_q_own, cross_kv_own = cross_weights
    cross_gain = gains[1]
    cross_blocks = jnp.concatenate(
        [
            (cross_q_own.astype(F32) * cross_gain[:, None]).astype(BF).reshape(own_rows, 1, 4, -1),
            cross_kv_own.reshape(own_rows, 2, 4, -1),
        ],
        axis=1,
    )
    cross_parts = jnp.moveaxis(cross_blocks, 2, 0).reshape(4, own_rows, -1)
    cross_parts = lax.all_to_all(cross_parts, four, 0, 0, tiled=True)
    cross_column = gather_z(after(cross_parts.reshape(4 * own_rows, -1), outs_column))
    gate_own = (after(w_gate_up, cross_parts).astype(F32) * gains[2][:, None]).astype(BF)
    gate_parts = gate_own.reshape(own_rows, 2, 2, z_count, 4, hidden_own)
    gate_parts = jnp.transpose(gate_parts, (2, 4, 0, 1, 3, 5)).reshape(8, own_rows, -1)
    gate_parts = lax.all_to_all(gate_parts, eight, 0, 0, tiled=True)
    gate_column = gather_z(after(gate_parts.reshape(8 * own_rows, -1), cross_column))
    down_full = gather_z(after(w_down, gate_column))
    qkv_full = attention_rows(qkv_column, own_rows)
    outs_column = outs_column.reshape(z_count, 2, own_rows, width)
    self_out_full = head_rows(outs_column[:, 0], own_rows)
    cross_full = attention_rows(cross_column, own_rows)
    cross_q_full, cross_kv_full = cross_full[:, :part], cross_full[:, part:]
    cross_out_full = head_rows(outs_column[:, 1], own_rows)
    gate_up_full = jnp.moveaxis(gate_column.reshape(z_count, 2, 4 * own_rows, -1), 0, 1).reshape(width, -1)
    hidden_units = down_full.shape[0]

    x_rows = tokens.astype(F32)
    norm_first = layer_norm(gather_four(tokens).astype(F32))
    projected = jnp.dot(norm_first, qkv_full, preferred_element_type=F32)
    tables = [key_position, cosine, down, up]
    query_rot, keys_rot, values_low, self_mixed, self_logsum = attention_call(
        self_forward_kernel,
        seq_two,
        tables,
        pairs,
        [(projected, span, 0), (projected, span, pairs), (projected, span, 2 * pairs)],
        [(span, BF)] * 4 + [(span, F32)],
        "self_forward",
    )
    self_branch = reduce_four(jnp.dot(self_mixed, self_out_full, preferred_element_type=F32), rows)
    after_self = x_rows + self_branch

    norm_second = gather_four(layer_norm(after_self))
    cross_query = jnp.dot(norm_second, cross_q_full, preferred_element_type=F32).astype(BF)
    cond_both = jnp.concatenate([conditioning, swap(conditioning, "c")], axis=0)
    cond_proj = jnp.dot(cond_both, cross_kv_full, preferred_element_type=F32).astype(BF)
    cross_mixed, cross_logsum = attention_call(
        cross_forward_kernel,
        cond_two,
        [cond_position],
        pairs,
        [(cross_query, span, 0), (cond_proj, cond_rows, 0), (cond_proj, cond_rows, pairs)],
        [(span, BF), (span, F32)],
        "cross_forward",
    )
    cross_branch = reduce_four(jnp.dot(cross_mixed, cross_out_full, preferred_element_type=F32), rows)
    after_cross = after_self + cross_branch

    norm_third = gather_eight(layer_norm(after_cross))
    grads_all = gather_eight(out_grad)
    gate_up = jnp.dot(norm_third, gate_up_full, preferred_element_type=F32)
    gate, upper = gate_up[:, :hidden_units], gate_up[:, hidden_units:]
    sig = jax.nn.sigmoid(gate)
    hidden = (gate * sig * upper).astype(BF)
    mlp_branch = reduce_eight(jnp.dot(hidden, down_full, preferred_element_type=F32), rows)
    block_sum = after_cross + mlp_branch
    square_terms = jnp.stack(
        [
            masked_square(value, row_valid)
            for value in (self_branch, after_self, cross_branch, after_cross, mlp_branch, block_sum)
        ]
    )

    grad_hidden = nt(grads_all, down_full)
    grad_gate = grad_hidden * upper * (sig * (1.0 + gate * (1.0 - sig)))
    grad_up = grad_hidden * (gate * sig)
    grad_gate_up = jnp.concatenate([grad_gate, grad_up], axis=1).astype(BF)
    grad_norm_third = reduce_eight(nt(grad_gate_up, gate_up_full), rows)
    d_down = scatter_z(tn(hidden, grads_all).astype(BF)).astype(F32)
    half_width = width // 2
    gate_grads = [
        scatter_z(tn(norm_third[:, s * half_width : (s + 1) * half_width], grad_gate_up).astype(BF))
        for s in range(2)
    ]
    gate_grads = jnp.concatenate(gate_grads, axis=0).reshape(8, own_rows, -1)
    gate_grads = lax.all_to_all(gate_grads, eight, 0, 0, tiled=True)
    gate_grads = gate_grads.reshape(2, 4, own_rows, 2, z_count, hidden_own)
    gate_grads = jnp.transpose(gate_grads, (2, 3, 0, 4, 1, 5)).reshape(own_rows, -1).astype(F32)
    d_gate_up, gain_third = gained(gate_grads, w_gate_up, gains[2])
    grad_after_cross = out_grad.astype(F32) + layer_norm_back(after_cross, grad_norm_third)

    cross_grad = gather_four(grad_after_cross.astype(BF))
    d_cross_out = head_rows_back(tn(cross_mixed, cross_grad))
    grad_cross_mixed = nt(cross_grad, cross_out_full).astype(BF)
    grad_cross_query, grad_cond_keys, grad_cond_values = attention_call(
        cross_backward_kernel,
        cond_two,
        [cond_position],
        pairs,
        [
            (cross_query, span, 0),
            (cond_proj, cond_rows, 0),
            (cond_proj, cond_rows, pairs),
            (cross_logsum, span, 0),
            (grad_cross_mixed, span, 0),
        ],
        [(span, BF), (cond_rows, BF), (cond_rows, BF)],
        "cross_backward",
    )
    grad_norm_second = reduce_four(nt(grad_cross_query, cross_q_full), rows)
    grad_cond = jnp.concatenate([grad_cond_keys, grad_cond_values], axis=1)
    cross_grads = jnp.concatenate([tn(norm_second, grad_cross_query), tn(cond_both, grad_cond)], axis=1)
    cross_grads = attention_rows_back(cross_grads, four)
    d_cross_q, gain_second = gained(cross_grads[:, 0], w_cross_q, gains[1])
    d_cross_kv = cross_grads[:, 1:].reshape(own_rows, -1)
    cond_back = nt(grad_cond, cross_kv_full).reshape(2, cond_rows, width)
    cond_back = cond_back[0] + swap(cond_back[1].astype(BF), "c").astype(F32)
    d_conditioning = cond_back.astype(BF).astype(F32) + swap(cond_back.astype(BF), "s").astype(F32)
    grad_after_self = grad_after_cross + layer_norm_back(after_self, grad_norm_second)

    self_grad = gather_four(grad_after_self.astype(BF))
    d_self_out = head_rows_back(tn(self_mixed, self_grad))
    grad_self_mixed = nt(self_grad, self_out_full).astype(BF)
    grad_proj = jnp.concatenate(
        attention_call(
            self_backward_kernel,
            seq_two,
            tables,
            pairs,
            [
                (query_rot, span, 0),
                (keys_rot, span, 0),
                (values_low, span, 0),
                (self_logsum, span, 0),
                (grad_self_mixed, span, 0),
            ],
            [(span, BF)] * 3,
            "self_backward",
        ),
        axis=1,
    )
    qkv_grads = attention_rows_back(tn(norm_first, grad_proj), four).reshape(own_rows, -1)
    d_qkv, gain_first = gained(qkv_grads, w_qkv, gains[0])
    grad_norm_first = reduce_four(nt(grad_proj, qkv_full), rows)
    grad_tokens = grad_after_self + layer_norm_back(x_rows, grad_norm_first)

    gain_own = jnp.stack([gain_first, gain_second, gain_third])
    valid_count = jnp.sum(seq_lengths).astype(F32)
    rms_stats = jnp.sqrt(lax.psum(square_terms, ALL) / (valid_count * width))
    return (
        block_sum.astype(BF),
        grad_tokens,
        d_conditioning,
        gain_own,
        d_qkv,
        d_self_out,
        d_cross_q,
        d_cross_kv,
        d_cross_out,
        d_gate_up,
        d_down,
        rms_stats,
    )


def solution(mesh):
    seq_count, fsdp_count = mesh.devices.shape
    fine = Mesh(mesh.devices.reshape(seq_count, fsdp_count // 4, 2, 2), ALL)
    by_token = P(("z", "y", "c", "s"), None)
    by_sequence = P(("z", "y", "c"), None)
    by_row = P(ALL, None)
    by_column = P(None, ALL)
    return jax.shard_map(
        shards,
        mesh=fine,
        in_specs=(by_token, by_sequence, P(), P(), by_column) + (by_row,) * 7 + (by_token,),
        out_specs=(by_token, by_token, by_sequence, by_column) + (by_row,) * 7 + (P(),),
        check_vma=False,
    )
```

```python
import functools
import math

import jax
import jax.numpy as jnp
from jax import lax
from jax.experimental import pallas as pl
from jax.experimental.pallas import tpu as pltpu
from jax.sharding import Mesh, PartitionSpec as P

HD = 64
LANES = 128
BF = jnp.bfloat16
F32 = jnp.float32
ALL = ("s", "z", "y", "c")


def nt(left, right):
    return lax.dot_general(left, right, (((1,), (1,)), ((), ())), preferred_element_type=F32)


def tn(left, right):
    return lax.dot_general(left, right, (((0,), (0,)), ((), ())), preferred_element_type=F32)


def nn(left, right):
    return lax.dot_general(left, right, (((1,), (0,)), ((), ())), preferred_element_type=F32)


def swap(value, axis):
    return lax.ppermute(value, axis, [(0, 1), (1, 0)])


def after(value, earlier):
    return lax.optimization_barrier((value, earlier))[0]


def gather_z(value):
    return lax.all_gather(value, "z", axis=0, tiled=True)


def scatter_z(value):
    return lax.psum_scatter(value, "z", scatter_dimension=0, tiled=True)


def cost(micros):
    return pl.CostEstimate(
        flops=int(1024 + micros * 1e9), transcendentals=0, bytes_accessed=int(1024 + micros * 3e6)
    )


def assemble_kernel(moves, *refs):
    sources, target = refs[:-1], refs[-1]
    for source, start, offset, size in moves:
        target[offset : offset + size] = sources[source][start : start + size]


def assemble(sources, moves, total, micros=0):
    width = sources[0].shape[1]
    column = 384 if width % 384 == 0 else width

    def block(height):
        return pl.BlockSpec((height, column), lambda j: (0, j))

    return pl.pallas_call(
        functools.partial(assemble_kernel, tuple(moves)),
        out_shape=jax.ShapeDtypeStruct((total, width), sources[0].dtype),
        grid=(width // column,),
        in_specs=[block(source.shape[0]) for source in sources],
        out_specs=block(total),
        compiler_params=pltpu.CompilerParams(vmem_limit_bytes=48 << 20),
        cost_estimate=cost(micros),
        name="assemble",
    )(*sources)


def gather_eight(low, high, micros=0, earlier=None):
    half = low.shape[0]
    s_high, y_low = swap(high, "s"), swap(low, "y")
    s_low, y_high = swap(low, "s"), swap(high, "y")
    if earlier is None:
        far_low, far_high = swap(y_low, "s"), swap(s_high, "y")
    else:
        far_low, far_high = swap(after(y_low, earlier), "s"), swap(after(s_high, earlier), "y")
    pieces = [high, s_high, s_low, low, y_low, far_low, far_high, y_high]
    here = assemble(pieces, [(i, 0, i * half, half) for i in range(8)], 8 * half, micros)
    return (here, swap(here, "c")), (y_low, s_high, s_low, y_high)


def half_positions(s_rank, rows):
    half = rows // 2
    step = jnp.arange(half, dtype=jnp.int32)
    mine, across = s_rank * rows + step, (1 - s_rank) * rows + step
    return jnp.stack(
        [
            jnp.concatenate([mine + half, across + half, across, mine]),
            jnp.concatenate([mine, across, across + half, mine + half]),
        ]
    )


def project_kernel(form, merged, value, weight, *refs):
    product = form(value[...], weight[...])
    if not merged:
        refs[0][...] = product.astype(refs[0].dtype)
        return
    product = product + refs[0][...].astype(F32)
    half = refs[1].shape[0]
    for index, block in enumerate((3, 4, 0, 1, 2, 5, 7, 6)):
        out = refs[1 + index]
        out[...] = product[block * half : (block + 1) * half].astype(out.dtype)


def project(value, weight, form, width, received=None, row_block=0, micros=0):
    rows, depth = value.shape
    column = 384
    weight_block = (
        pl.BlockSpec((depth, column), lambda j: (row_block, j))
        if form is nn
        else pl.BlockSpec((column, depth), lambda j: (j, 0))
    )

    def block(height):
        return pl.BlockSpec((height, column), lambda j: (0, j))

    merged = received is not None
    if merged:
        outs = [jax.ShapeDtypeStruct((rows // 8, width), F32 if i < 4 else BF) for i in range(8)]
    else:
        outs = [jax.ShapeDtypeStruct((rows, width), BF)]
    return pl.pallas_call(
        functools.partial(project_kernel, form, merged),
        out_shape=outs,
        grid=(width // column,),
        in_specs=[pl.BlockSpec((rows, depth), lambda j: (0, 0)), weight_block] + [block(rows)] * merged,
        out_specs=[block(o.shape[0]) for o in outs],
        compiler_params=pltpu.CompilerParams(vmem_limit_bytes=48 << 20),
        cost_estimate=cost(micros),
        name="project",
    )(value, weight, *([received] if merged else []))


def project_last_kernel(grads, weight, received, hidden, down_weight, down_received, *outs):
    products = (
        nt(grads[...], weight[...]) + received[...].astype(F32),
        nn(hidden[...], down_weight[...]) + down_received[...].astype(F32),
    )
    half = outs[0].shape[0] // 2
    for index, block in enumerate((3, 4, 0, 1, 2, 5, 7, 6)):
        for side, product in enumerate(products):
            outs[index][side * half : (side + 1) * half] = product[block * half : (block + 1) * half].astype(
                outs[index].dtype
            )


def project_last(grads, weight, received, hidden, ff_weight, down_received):
    rows, width = received.shape
    column = 384
    row_block = width // hidden.shape[1]

    def block(height):
        return pl.BlockSpec((height, column), lambda j: (0, j))

    def whole(value):
        return pl.BlockSpec(value.shape, lambda j: (0, 0))

    return pl.pallas_call(
        project_last_kernel,
        out_shape=[jax.ShapeDtypeStruct((rows // 4, width), F32 if i < 4 else BF) for i in range(8)],
        grid=(width // column,),
        in_specs=[
            whole(grads),
            pl.BlockSpec((column, weight.shape[1]), lambda j: (j, 0)),
            block(rows),
            whole(hidden),
            pl.BlockSpec((hidden.shape[1], column), lambda j: (row_block, j)),
            block(rows),
        ],
        out_specs=[block(rows // 4)] * 8,
        compiler_params=pltpu.CompilerParams(vmem_limit_bytes=48 << 20),
        cost_estimate=cost(9),
        name="project_last",
    )(grads, weight, received, hidden, ff_weight, down_received)


def add_kernel(left, right, out):
    out[...] = (left[...] + right[...].astype(F32)).astype(BF)


def add_low(left, right, micros=0):
    return pl.pallas_call(
        add_kernel,
        out_shape=jax.ShapeDtypeStruct(left.shape, BF),
        cost_estimate=cost(micros),
        name="add_low",
    )(left, right)


def reduce_eight(blocks, micros=0):
    own_low, y_low, own_high, s_high, to_s, to_s_far, to_y, to_y_far = blocks
    got_far_low, got_far_high = swap(to_s_far, "s"), swap(to_y_far, "y")
    got_low, got_high = swap(to_s, "s"), swap(to_y, "y")
    sum_low, sum_high = add_low(y_low, got_far_low, micros), add_low(s_high, got_far_high, micros)
    parts = (own_low, got_low, swap(sum_low, "y")), (own_high, got_high, swap(sum_high, "s"))
    return parts, (sum_low, sum_high, got_low, got_high)


def sum_everywhere(total):
    for axis in ("c", "y", "s"):
        total = total + swap(total, axis)
    z_count = lax.axis_size("z")
    step = 1
    while step < z_count:
        total = total + lax.ppermute(total, "z", [(i, i ^ step) for i in range(z_count)])
        step *= 2
    return total


def slab(weight):
    rows = weight.shape[0]
    parts = jnp.moveaxis(weight.reshape(rows, 3, 8, -1), 2, 0)
    split = 2 * HD
    return jnp.concatenate(
        [parts[..., :split].reshape(8, rows, -1), parts[..., split:].reshape(8, rows, -1)], axis=-1
    )


def unslab(parts):
    rows = parts.shape[1]
    split = 6 * HD
    merged = jnp.concatenate(
        [parts[..., :split].reshape(8, rows, 3, -1), parts[..., split:].reshape(8, rows, 3, -1)], axis=-1
    )
    return jnp.moveaxis(merged, 0, 2).reshape(rows, -1)


def cross_slab(query, keys_values):
    rows = query.shape[0]
    query = query.reshape(rows, 8, -1)
    keys_values = keys_values.reshape(rows, 2, 8, -1)
    keys, values = keys_values[:, 0], keys_values[:, 1]
    split = 2 * HD
    parts = [keys[..., :split], values[..., :split], keys[..., split:], values[..., split:], query]
    return jnp.moveaxis(jnp.concatenate(parts, axis=-1), 1, 0)


def cross_unslab(parts):
    rows = parts.shape[1]
    parts = jnp.moveaxis(parts, 0, 1)
    keys = jnp.concatenate([parts[..., :128], parts[..., 256:320]], axis=-1)
    values = jnp.concatenate([parts[..., 128:256], parts[..., 320:384]], axis=-1)
    keys_values = jnp.concatenate([keys.reshape(rows, -1), values.reshape(rows, -1)], axis=1)
    return parts[..., 384:].reshape(rows, -1), keys_values


def model_rows(column, rows, width, more=0):
    z_count = lax.axis_size("z")
    stride = column.shape[0] // z_count
    part = 4 * rows
    moves = [
        (0, z * stride + s * part, (s * z_count + z) * part, part) for s in range(2) for z in range(z_count)
    ]
    moves += [(0, z * stride + 2 * part, width + z * more, more) for z in range(z_count) if more]
    return assemble([column], moves, width + z_count * more)


def permute_back(value):
    z_count = lax.axis_size("z")
    part = z_count // 4
    pairs = []
    for z in range(z_count):
        for corner in range(4):
            triple, step = divmod(z, part)
            pairs.append(((step * 4 + corner) * 4 + triple, z * 4 + corner))
    return lax.ppermute(value, ("z", "y", "c"), pairs)


def gained(grad, weight, gain):
    return grad * gain[:, None], jnp.sum(grad * weight.astype(F32), axis=1)


def head_masks(shape):
    lane = lax.broadcasted_iota(jnp.int32, shape, 1)
    return lane < HD


def rotate(values, cos_ref, down_ref, up_ref, sign):
    ahead = pltpu.roll(values, LANES - 16, 1)
    behind = pltpu.roll(values, 16, 1)
    return values * cos_ref[...] + sign * (ahead * down_ref[...] + behind * up_ref[...])


def forward_heads(query, keys, values, valid):
    left = head_masks(query.shape)
    outs, logs = [], []
    for head in range(2):
        picked = left if head == 0 else jnp.logical_not(left)
        scores = nt(jnp.where(picked, query, jnp.zeros_like(query)), keys) * 0.125
        scores = jnp.where(valid, scores, -1e30)
        peak = jnp.max(scores, axis=-1, keepdims=True)
        expo = jnp.exp(scores - peak)
        total = jnp.sum(expo, axis=-1, keepdims=True)
        probs = (expo * (1.0 / total)).astype(BF)
        outs.append(nn(probs, values))
        logs.append(peak + jnp.log(total))
    return (
        jnp.where(left, outs[0], outs[1]).astype(BF),
        jnp.where(left, logs[0], logs[1]),
    )


def backward_heads(query, keys, values, valid, logsum, grad):
    left = head_masks(query.shape)
    left_keys = head_masks(keys.shape)
    grad_q, grad_k, grad_v = [], [], []
    for head in range(2):
        picked = left if head == 0 else jnp.logical_not(left)
        none = jnp.zeros_like(query)
        scores = nt(jnp.where(picked, query, none), keys) * 0.125
        scores = jnp.where(valid, scores, -1e30)
        probs = jnp.exp(scores - logsum[:, head * HD : head * HD + 1])
        grad_probs = nt(jnp.where(picked, grad, none), values)
        delta = jnp.sum(probs * grad_probs, axis=-1, keepdims=True)
        grad_scores = (probs * (grad_probs - delta)).astype(BF)
        grad_q.append(nn(grad_scores, keys))
        grad_k.append(tn(grad_scores, query))
        grad_v.append(tn(probs.astype(BF), grad))
    return (
        jnp.where(left, grad_q[0], grad_q[1]) * 0.125,
        jnp.where(left_keys, grad_k[0], grad_k[1]) * 0.125,
        jnp.where(left_keys, grad_v[0], grad_v[1]),
    )


def one_head(query, keys, values, valid):
    scores = jnp.where(valid, nt(query, keys) * 0.125, -1e30)
    peak = jnp.max(scores, axis=-1, keepdims=True)
    expo = jnp.exp(scores - peak)
    total = jnp.sum(expo, axis=-1, keepdims=True)
    return nn((expo * (1.0 / total)).astype(BF), values), peak + jnp.log(total)


def one_head_back(query, keys, values, valid, logsum, grad):
    scores = jnp.where(valid, nt(query, keys) * 0.125, -1e30)
    probs = jnp.exp(scores - logsum)
    grad_probs = nt(grad, values)
    delta = jnp.sum(probs * grad_probs, axis=-1, keepdims=True)
    return (probs * (grad_probs - delta)).astype(BF), probs.astype(BF)


def one_head(query, keys, values, valid):
    scores = jnp.where(valid, nt(query, keys) * 0.125, -1e30)
    peak = jnp.max(scores, axis=-1, keepdims=True)
    expo = jnp.exp(scores - peak)
    total = jnp.sum(expo, axis=-1, keepdims=True)
    return nn((expo * (1.0 / total)).astype(BF), values), peak + jnp.log(total)


def one_head_back(query, keys, values, valid, logsum, grad):
    scores = jnp.where(valid, nt(query, keys) * 0.125, -1e30)
    probs = jnp.exp(scores - logsum)
    grad_probs = nt(grad, values)
    delta = jnp.sum(probs * grad_probs, axis=-1, keepdims=True)
    return (probs * (grad_probs - delta)).astype(BF), probs.astype(BF)


def self_forward_kernel(
    lengths, position, cosine, down, up, rows, weight, rotated, mixed, logsum
):
    projected = nn(rows[...], weight[...])
    pieces = [rotate(projected[:, i : i + LANES], cosine, down, up, 1.0).astype(BF) for i in (0, 128, 384)]
    values = projected[:, 256:384].astype(BF)
    values_last = projected[:, 512:576].astype(BF)
    rotated[:, 0:128] = pieces[0]
    rotated[:, 128:256] = pieces[1]
    rotated[:, 256:384] = values
    rotated[:, 384:512] = pieces[2]
    rotated[:, 512:576] = values_last
    valid = position[0:1, :] < lengths[pl.program_id(0)]
    mixed_pair, logsum_pair = forward_heads(pieces[0], pieces[1], values, valid)
    mixed[:, 0:128] = mixed_pair
    logsum[:, 0:128] = logsum_pair
    last = pieces[2]
    left = head_masks(last.shape)
    mixed_last, logsum_last = one_head(
        jnp.where(left, last, jnp.zeros_like(last)), pltpu.roll(last, HD, 1), values_last, valid
    )
    mixed[:, 128:192] = mixed_last.astype(BF)
    logsum[:, 128:192] = jnp.broadcast_to(logsum_last, mixed_last.shape)


def self_backward_kernel(
    lengths, position, cosine, down, up, rotated, logsum, grad_rows, weight, out_weight, grad_out, *partial
):
    grad = nt(grad_rows[...], out_weight[...]).astype(BF)
    valid = position[0:1, :] < lengths[pl.program_id(0)]
    back_q, back_k, back_v = backward_heads(
        rotated[:, 0:128], rotated[:, 128:256], rotated[:, 256:384], valid, logsum[:, 0:128], grad[:, 0:128]
    )
    grad_out[:, 0:128] = rotate(back_q, cosine, down, up, -1.0).astype(BF)
    grad_out[:, 128:256] = rotate(back_k, cosine, down, up, -1.0).astype(BF)
    grad_out[:, 256:384] = back_v.astype(BF)
    last = rotated[:, 384:512]
    turned = pltpu.roll(last, HD, 1)
    left = head_masks(last.shape)
    grad_last = grad[:, 128:192]
    grad_scores, probs = one_head_back(
        jnp.where(left, last, jnp.zeros_like(last)),
        turned,
        rotated[:, 512:576],
        valid,
        logsum[:, 128:129],
        grad_last,
    )
    both = jnp.where(left, nn(grad_scores, turned), pltpu.roll(tn(grad_scores, last), HD, 1)) * 0.125
    grad_out[:, 384:512] = rotate(both, cosine, down, up, -1.0).astype(BF)
    grad_out[:, 512:576] = tn(probs, grad_last).astype(BF)
    for out in partial:
        out[...] = nt(grad_out[...], weight[...]).astype(BF)


def cross_forward_kernel(
    lengths, position, rows, keys_values, weight, out_weight, query, mixed, logsum, *partial
):
    query[...] = nn(rows[...], weight[...]).astype(BF)
    valid = position[0:1, :] < lengths[pl.program_id(0)]
    mixed_pair, logsum_pair = forward_heads(
        query[:, 0:128], keys_values[:, 0:128], keys_values[:, 128:256], valid
    )
    mixed[:, 0:128] = mixed_pair
    logsum[:, 0:128] = logsum_pair
    last = keys_values[:, 256:384]
    values = pltpu.roll(last, HD, 1)[:, 0:HD]
    mixed_last, logsum_last = one_head(query[:, 128:192], last[:, 0:HD], values, valid)
    mixed[:, 128:192] = mixed_last.astype(BF)
    logsum[:, 128:192] = jnp.broadcast_to(logsum_last, mixed_last.shape)
    for out in partial:
        out[...] = nn(mixed[...], out_weight[...]).astype(BF)


def cross_backward_kernel(
    lengths, position, query, keys_values, logsum, grad_rows, weight, out_weight, grad_q, grad_kv, *partial
):
    grad = nt(grad_rows[...], out_weight[...]).astype(BF)
    valid = position[0:1, :] < lengths[pl.program_id(0)]
    back_q, back_k, back_v = backward_heads(
        query[:, 0:128], keys_values[:, 0:128], keys_values[:, 128:256], valid, logsum[:, 0:128], grad[:, 0:128]
    )
    grad_q[:, 0:128] = back_q.astype(BF)
    grad_kv[:, 0:128] = back_k.astype(BF)
    grad_kv[:, 128:256] = back_v.astype(BF)
    last = keys_values[:, 256:384]
    keys = last[:, 0:HD]
    query_last, grad_last = query[:, 128:192], grad[:, 128:192]
    grad_scores, probs = one_head_back(
        query_last, keys, pltpu.roll(last, HD, 1)[:, 0:HD], valid, logsum[:, 128:129], grad_last
    )
    grad_q[:, 128:192] = (nn(grad_scores, keys) * 0.125).astype(BF)
    grad_kv[:, 256:384] = jnp.concatenate(
        [tn(grad_scores, query_last) * 0.125, tn(probs, grad_last)], axis=1
    ).astype(BF)
    for out in partial:
        out[...] = nt(grad_q[...], weight[...]).astype(BF)


def attention_call(kernel, lengths, tables, inputs, weights, outputs, name, micros=0):
    sequences = lengths.shape[0]

    def block(rows, width):
        return pl.BlockSpec((rows // sequences, width), lambda b, ln: (b, 0))

    def table(value):
        return pl.BlockSpec((None,) + value.shape[1:], lambda b, ln: (b, 0, 0))

    def whole(value):
        return pl.BlockSpec(value.shape, lambda b, ln: (0, 0))

    return pl.pallas_call(
        kernel,
        out_shape=[jax.ShapeDtypeStruct((r, w), dt) for r, w, dt in outputs],
        grid_spec=pltpu.PrefetchScalarGridSpec(
            num_scalar_prefetch=1,
            grid=(sequences,),
            in_specs=[table(t) for t in tables]
            + [block(*i.shape) for i in inputs]
            + [whole(w) for w in weights],
            out_specs=[block(r, w) for r, w, _ in outputs],
        ),
        compiler_params=pltpu.CompilerParams(
            dimension_semantics=("arbitrary",), vmem_limit_bytes=48 << 20
        ),
        cost_estimate=cost(micros),
        name=name,
    )(lengths, *tables, *inputs, *weights)


def feed_forward_kernel(rows, grad_rows, weights, hidden, grad_out, *partial):
    units, width = hidden.shape[1], rows.shape[1]
    gate = nn(rows[...], weights[:width, :units])
    upper = nn(rows[...], weights[:width, units:])
    sig = jax.nn.sigmoid(gate)
    silu = gate * sig
    hidden[...] = (silu * upper).astype(BF)
    grad_hidden = nt(grad_rows[...], weights[width:])
    grad_out[:, :units] = (grad_hidden * upper * (sig * (1.0 + gate * (1.0 - sig)))).astype(BF)
    grad_out[:, units:] = (grad_hidden * silu).astype(BF)
    for out in partial:
        out[...] = nt(grad_out[...], weights[:width]).astype(BF)


def feed_forward(rows, grad_rows, weights, partial):
    total, width = rows.shape
    units = weights.shape[1] // 2
    block = total // 2

    def whole(value):
        return pl.BlockSpec(value.shape, lambda i: (0, 0))

    widths = [units, 2 * units] + [width] * partial
    return pl.pallas_call(
        feed_forward_kernel,
        out_shape=[jax.ShapeDtypeStruct((total, w), BF) for w in widths],
        grid=(2,),
        in_specs=[pl.BlockSpec((block, width), lambda i: (i, 0))] * 2 + [whole(weights)],
        out_specs=[pl.BlockSpec((block, w), lambda i: (i, 0)) for w in widths],
        compiler_params=pltpu.CompilerParams(vmem_limit_bytes=56 << 20),
        cost_estimate=cost(10),
        name="feed_forward",
    )(rows, grad_rows, weights)


def weight_grad_kernel(here, there, grad_here, grad_there, out):
    grad = tn(here[...], grad_here[...]) + tn(there[...], grad_there[...])
    out[...] = grad.astype(BF).reshape(out.shape)


def weight_grad(rows, grads, own_rows=None):
    total, width = rows[0].shape
    columns = grads[0].shape[1]
    block = 3 * LANES
    steps = width // block
    if own_rows is None:
        out_shape, out_block = (width, columns), pl.BlockSpec((block, columns), lambda i: (i, 0))
    else:
        z_count, part = lax.axis_size("z"), 4 * own_rows
        turn = steps // 2
        out_shape = (z_count, 2, part, columns)
        out_block = pl.BlockSpec((block // part, None, part, columns), lambda i: (i % turn, i // turn, 0, 0))
    return pl.pallas_call(
        weight_grad_kernel,
        out_shape=jax.ShapeDtypeStruct(out_shape, BF),
        grid=(steps,),
        in_specs=[pl.BlockSpec((total, block), lambda i: (0, i))] * 2
        + [pl.BlockSpec((total, columns), lambda i: (0, 0))] * 2,
        out_specs=out_block,
        compiler_params=pltpu.CompilerParams(vmem_limit_bytes=48 << 20),
        cost_estimate=cost(total * width * columns / 2e8),
        name="weight_grad",
    )(*rows, *grads)


def spread_gate_kernel(unit, gain, weight, out):
    scaled = weight[...].astype(F32) * gain[...]
    corners, _, width = out.shape
    for z in range(width // unit):
        for corner in range(corners):
            start = (z * corners + corner) * unit
            out[corner, :, z * unit : (z + 1) * unit] = scaled[:, start : start + unit].astype(BF)


def spread_gate(weight, gain, unit):
    rows, columns = weight.shape
    quarter = columns // 4
    return pl.pallas_call(
        functools.partial(spread_gate_kernel, unit),
        out_shape=jax.ShapeDtypeStruct((8, rows, columns // 8), BF),
        grid=(2, 2),
        in_specs=[
            pl.BlockSpec((rows, 1), lambda g, s: (0, 0)),
            pl.BlockSpec((rows, quarter), lambda g, s: (0, 2 * g + s)),
        ],
        out_specs=pl.BlockSpec((4, rows, quarter // 4), lambda g, s: (s, 0, g)),
        cost_estimate=cost(0),
        name="spread_gate",
    )(gain[:, None], weight)


def collect_gate_kernel(unit, gain, weight, grads, out, sums):
    @pl.when((pl.program_id(0) == 0) & (pl.program_id(1) == 0))
    def _():
        sums[...] = jnp.zeros_like(sums)

    corners, rows, width = grads.shape
    total = jnp.zeros((rows, 1), F32)
    for z in range(width // unit):
        for corner in range(corners):
            cut = slice((z * corners + corner) * unit, (z * corners + corner + 1) * unit)
            grad = grads[corner, :, z * unit : (z + 1) * unit].astype(F32)
            out[:, cut] = grad * gain[...]
            total = total + jnp.sum(grad * weight[:, cut].astype(F32), axis=1, keepdims=True)
    sums[...] = sums[...] + total


def collect_gate(grads, weight, gain, unit):
    rows, columns = weight.shape
    quarter = columns // 4
    grad, sums = pl.pallas_call(
        functools.partial(collect_gate_kernel, unit),
        out_shape=[jax.ShapeDtypeStruct((rows, columns), F32), jax.ShapeDtypeStruct((rows, LANES), F32)],
        grid=(2, 2),
        in_specs=[
            pl.BlockSpec((rows, 1), lambda g, s: (0, 0)),
            pl.BlockSpec((rows, quarter), lambda g, s: (0, 2 * g + s)),
            pl.BlockSpec((4, rows, quarter // 4), lambda g, s: (s, 0, g)),
        ],
        out_specs=[
            pl.BlockSpec((rows, quarter), lambda g, s: (0, 2 * g + s)),
            pl.BlockSpec((rows, LANES), lambda g, s: (0, 0)),
        ],
        cost_estimate=cost(10),
        name="collect_gate",
    )(gain[:, None], weight, grads)
    return grad, sums[:, 0]


def normalize(hidden):
    centred = hidden - jnp.mean(hidden, axis=-1, keepdims=True)
    inverse = lax.rsqrt(jnp.mean(centred * centred, axis=-1, keepdims=True) + 1e-05)
    return centred * inverse, inverse


def layer_norm_back(hidden, scaled):
    unit, inverse = normalize(hidden)
    return inverse * (
        scaled
        - jnp.mean(scaled, axis=-1, keepdims=True)
        - unit * jnp.mean(scaled * unit, axis=-1, keepdims=True)
    )


def total_of(parts):
    return parts[0][...] + parts[1][...].astype(F32) + parts[2][...].astype(F32)


def lane_sums(value):
    sums = jnp.sum(value, axis=0, keepdims=True)
    return sum(sums[:, i : i + LANES] for i in range(0, sums.shape[1], LANES))


def forward_rows_kernel(bounds, stream, *refs):
    parts, (stream_out, low_out, high_out, squares) = (refs[:3], refs[3:6]), refs[6:]
    half = low_out.shape[0]
    sums = [0.0, 0.0]
    for index, out in enumerate((low_out, high_out)):
        rows = slice(index * half, (index + 1) * half)
        branch = total_of(parts[index])
        hidden = stream[rows] + branch
        stream_out[rows] = hidden
        out[...] = normalize(hidden)[0].astype(BF)
        position = bounds[0] + index * half + lax.broadcasted_iota(jnp.int32, (half, 1), 0)
        weight = jnp.where(position < bounds[1], 1.0, 0.0)
        sums = [sums[0] + lane_sums(branch * branch * weight), sums[1] + lane_sums(hidden * hidden * weight)]
    squares[0:1] = sums[0]
    squares[1:2] = sums[1]


def last_rows_kernel(bounds, stream, grad, inputs, *refs):
    parts, (grad_out, stream_out, squares) = (refs[:3], refs[3:6]), refs[6:]
    half = stream.shape[0] // 2
    sums = [0.0, 0.0]
    for index in range(2):
        rows = slice(index * half, (index + 1) * half)
        both = total_of(parts[index])
        grad_out[rows] = grad[rows] + layer_norm_back(inputs[rows].astype(F32), both[:half])
        branch = both[half:]
        hidden = stream[rows] + branch
        stream_out[rows] = hidden.astype(BF)
        position = bounds[0] + index * half + lax.broadcasted_iota(jnp.int32, (half, 1), 0)
        weight = jnp.where(position < bounds[1], 1.0, 0.0)
        sums = [sums[0] + lane_sums(branch * branch * weight), sums[1] + lane_sums(hidden * hidden * weight)]
    squares[0:1] = sums[0]
    squares[1:2] = sums[1]


def backward_rows_kernel(grad, stream, *refs):
    parts, outs = (refs[:3], refs[3:6]), refs[6:]
    half = parts[0][0].shape[0]
    for index in range(2):
        rows = slice(index * half, (index + 1) * half)
        total = grad[rows].astype(F32) + layer_norm_back(stream[rows].astype(F32), total_of(parts[index]))
        outs[0][rows] = total
        if len(outs) > 1:
            outs[1 + index][...] = total.astype(BF)


def rows_call(kernel, leading, parts, outputs, name, micros=0):
    vmem = pl.BlockSpec(memory_space=pltpu.VMEM)
    smem = pl.BlockSpec(memory_space=pltpu.SMEM)
    operands = list(leading) + list(parts[0]) + list(parts[1])
    return pl.pallas_call(
        kernel,
        out_shape=[jax.ShapeDtypeStruct(shape, dt) for shape, dt in outputs],
        in_specs=[smem if o.ndim == 1 else vmem for o in operands],
        out_specs=[vmem] * len(outputs),
        compiler_params=pltpu.CompilerParams(vmem_limit_bytes=48 << 20),
        cost_estimate=cost(micros),
        name=name,
    )(*operands)


def shards(
    tokens,
    conditioning,
    seq_lengths,
    cond_lengths,
    norm_gains,
    w_qkv,
    w_self_out,
    w_cross_q,
    w_cross_kv,
    w_cross_out,
    w_gate_up,
    w_down,
    out_grad,
):
    rows, width = tokens.shape
    half = rows // 2
    z_count = lax.axis_size("z")
    own_rows = w_qkv.shape[0]
    hidden_own = w_down.shape[0]
    s_rank, z_rank = lax.axis_index("s"), lax.axis_index("z")
    y_rank, c_rank = lax.axis_index("y"), lax.axis_index("c")
    span = 2 * rows

    first_seq = (z_rank * 2 + y_rank) * 2
    mine, other = first_seq + c_rank, first_seq + 1 - c_rank
    across, corner = (z_rank * 2 + 1 - y_rank) * 2 + c_rank, (z_rank * 2 + 1 - y_rank) * 2 + 1 - c_rank
    seq_here = jnp.stack([seq_lengths[mine], seq_lengths[across]])
    seq_there = jnp.stack([seq_lengths[other], seq_lengths[corner]])
    cond_here_lengths = jnp.stack([cond_lengths[mine], cond_lengths[across]])
    cond_there_lengths = jnp.stack([cond_lengths[other], cond_lengths[corner]])
    bounds = jnp.stack([s_rank * rows, seq_lengths[mine]])
    positions = half_positions(s_rank, rows)
    lane = jnp.arange(LANES, dtype=jnp.int32) % HD
    freqs = jnp.exp((lane % 16).astype(F32) * (-math.log(10000.0) / 16.0))
    angles = positions.astype(F32)[..., None] * freqs
    cosine = jnp.where(lane < 32, jnp.cos(angles), 1.0)
    sine = jnp.sin(angles)
    down = jnp.where(lane < 16, -sine, 0.0)
    up = jnp.where((lane >= 16) & (lane < 32), sine, 0.0)
    tables = [jnp.broadcast_to(positions[:, None, :], (2, 8, span)), cosine, down, up]
    cond_rows = conditioning.shape[0]
    cond_position = jnp.broadcast_to(jnp.arange(cond_rows, dtype=jnp.int32), (2, 8, cond_rows))

    eight = ("s", "y", "c")
    gains = norm_gains.astype(F32)
    qkv_parts = slab((w_qkv.astype(F32) * gains[0][:, None]).astype(BF))
    qkv_parts = lax.all_to_all(qkv_parts, eight, 0, 0, tiled=True)
    slab_width = qkv_parts.shape[-1]
    head_width = slab_width // 3
    slab_rows = 8 * own_rows

    def out_rows(column):
        column = column.reshape(z_count, -1, slab_width)[:, slab_rows:].reshape(4, -1, own_rows, width)
        column = lax.all_to_all(column, ("y", "c"), 0, 0, tiled=True)
        return jnp.moveaxis(column, 0, 1).reshape(-1, width)

    qkv_both = jnp.concatenate([qkv_parts.reshape(slab_rows, -1), w_self_out.reshape(-1, slab_width)], axis=0)
    qkv_column = gather_z(qkv_both)
    conditioning, cross_q_own, cross_kv_own = after((conditioning, w_cross_q, w_cross_kv), qkv_both)
    cond_here = jnp.concatenate([conditioning, swap(conditioning, "y")], axis=0)
    cond = (cond_here, swap(cond_here, "c"))
    cross_parts = cross_slab((cross_q_own.astype(F32) * gains[1][:, None]).astype(BF), cross_kv_own)
    cross_parts = lax.all_to_all(cross_parts, eight, 0, 0, tiled=True)
    cross_both = jnp.concatenate([cross_parts.reshape(slab_rows, -1), w_cross_out.reshape(-1, slab_width)], axis=0)
    out_grads_all, _ = gather_eight(out_grad[:half], out_grad[half:], 0, qkv_both)
    gate_parts = spread_gate(after(w_gate_up, cross_parts), gains[2], hidden_own)
    gate_parts = lax.all_to_all(gate_parts, eight, 0, 0, tiled=True)
    tokens_now = after(tokens, (out_grads_all[0], cross_both, cond[0]))
    first_unit = normalize(tokens_now.astype(F32))[0].astype(BF)
    first, _ = gather_eight(first_unit[:half], first_unit[half:])
    cross_column = gather_z(after(cross_both, out_grads_all[0]))
    qkv_column = after(qkv_column, (first[0], gate_parts))
    qkv_full = model_rows(qkv_column, own_rows, width)
    self_out_full = out_rows(qkv_column)

    def self_attention(side, lengths):
        return attention_call(
            self_forward_kernel,
            lengths,
            tables,
            [first[side]],
            [qkv_full],
            [(2 * span, slab_width, BF), (2 * span, head_width, BF), (2 * span, head_width, F32)],
            "self_forward",
        )

    self_here = self_attention(0, seq_here)
    self_there = self_attention(1, seq_there)
    ff_column = gather_z(after(jnp.concatenate([gate_parts.reshape(slab_rows, -1), w_down], axis=0), qkv_full))
    (self_partial,) = project(self_there[1], self_out_full, nn, width)
    parts, sent = reduce_eight(project(self_here[1], self_out_full, nn, width, swap(self_partial, "c")))
    forward_outs = [((rows, width), F32), ((half, width), BF), ((half, width), BF), ((8, LANES), F32)]
    cross_column = after(cross_column, sent)
    cross_full = model_rows(cross_column, own_rows, width)
    kv_width = 2 * head_width
    cross_kv_full, cross_q_full = cross_full[:, :kv_width], cross_full[:, kv_width:]
    cross_out_full = out_rows(cross_column)
    cond_proj = [nn(c, cross_kv_full).astype(BF) for c in cond]
    parts = after(parts, (cond_proj, cross_q_full, cross_out_full))
    after_self, second_low, second_high, squares_self = rows_call(
        forward_rows_kernel, [bounds, tokens.astype(F32)], parts, forward_outs, "forward_rows"
    )

    second, _ = gather_eight(second_low, second_high)

    def cross_attention(side, lengths, partial):
        return attention_call(
            cross_forward_kernel,
            lengths,
            [cond_position],
            [second[side], cond_proj[side]],
            [cross_q_full, cross_out_full],
            [(2 * span, head_width, BF), (2 * span, head_width, BF), (2 * span, head_width, F32)]
            + [(2 * span, width, BF)] * partial,
            "cross_forward",
        )

    cross_there = cross_attention(1, cond_there_lengths, 1)
    cross_here = cross_attention(0, cond_here_lengths, 0)
    parts, sent = reduce_eight(project(cross_here[1], cross_out_full, nn, width, swap(cross_there[3], "c")))
    ff_full = model_rows(after(ff_column, sent), own_rows, width, hidden_own)
    parts = after(parts, ff_full)
    after_cross, third_low, third_high, squares_cross = rows_call(
        forward_rows_kernel, [bounds, after_self], parts, forward_outs, "forward_rows"
    )

    third, _ = gather_eight(third_low, third_high)
    hidden_there, gates_there, back_there = feed_forward(third[1], out_grads_all[1], ff_full, 1)
    hidden_here, gates_here = feed_forward(third[0], out_grads_all[0], ff_full, 0)
    parts, sent = reduce_eight(project(gates_here, ff_full, nt, width, swap(back_there, "c"), micros=8), 2)
    hidden_here, hidden_there, gates_here, gates_there = after(
        (hidden_here, hidden_there, gates_here, gates_there), sent
    )
    down_grad = weight_grad((hidden_here, hidden_there), out_grads_all)
    d_down = scatter_z(down_grad)
    parts = after(parts, down_grad)
    backward_outs = [((rows, width), F32), ((half, width), BF), ((half, width), BF)]
    grad_after_cross, cross_low, cross_high = rows_call(
        backward_rows_kernel, [out_grad, after_cross], parts, backward_outs, "backward_rows", 3
    )

    cross_grad, sent = gather_eight(cross_low, cross_high, 3)
    gate_grad = weight_grad(third, after((gates_here, gates_there), sent), own_rows)
    gate_grads = scatter_z(gate_grad.reshape(-1, gate_grad.shape[-1]))
    cross_grad = after(cross_grad, gate_grad)

    def cross_attention_back(side, forward, lengths, partial):
        return attention_call(
            cross_backward_kernel,
            lengths,
            [cond_position],
            [forward[0], cond_proj[side], forward[2], cross_grad[side]],
            [cross_q_full, cross_out_full],
            [(2 * span, head_width, BF), (2 * cond_rows, kv_width, BF)] + [(2 * span, width, BF)] * partial,
            "cross_backward",
            5,
        )

    back_there = cross_attention_back(1, cross_there, cond_there_lengths, 1)
    back_here = cross_attention_back(0, cross_here, cond_here_lengths, 0)
    parts, sent = reduce_eight(
        project(back_here[0], cross_q_full, nt, width, swap(back_there[2], "c"), micros=5), 2
    )
    back_queries, back_keys = after(((back_here[0], back_there[0]), (back_here[1], back_there[1])), sent)
    cross_grads = jnp.concatenate(
        [weight_grad(cond, back_keys, own_rows), weight_grad(second, back_queries, own_rows)], axis=-1
    )
    cross_out_grad = (tn(cross_here[1], cross_grad[0]) + tn(cross_there[1], cross_grad[1])).astype(BF)
    cross_grads = jnp.concatenate(
        [
            cross_grads.reshape(z_count, slab_rows, slab_width),
            cross_out_grad.reshape(z_count, own_rows, width).reshape(z_count, -1, slab_width),
        ],
        axis=1,
    )
    parts = after(parts, (cross_grads, d_down))
    cross_grads = scatter_z(cross_grads.reshape(-1, slab_width))
    cond_back = nt(back_here[1], cross_kv_full) + swap(nt(back_there[1], cross_kv_full).astype(BF), "c").astype(F32)
    cond_back = cond_back[:cond_rows] + swap(cond_back[cond_rows:].astype(BF), "y").astype(F32)
    d_conditioning = cond_back.astype(BF).astype(F32) + swap(cond_back.astype(BF), "s").astype(F32)
    grad_after_self, self_low, self_high = rows_call(
        backward_rows_kernel, [grad_after_cross, after_self], parts, backward_outs, "backward_rows", 3
    )

    self_grad, sent = gather_eight(self_low, self_high, 3)
    down_block = width // hidden_here.shape[1]
    (mlp_there,) = project(after(hidden_there, sent), ff_full, nn, width, None, down_block, 5)
    mlp_there = swap(mlp_there, "c")
    self_grad = after(self_grad, gate_grads)
    self_out_grad = (tn(self_here[1], self_grad[0]) + tn(self_there[1], self_grad[1])).astype(BF)
    d_self_out = scatter_z(self_out_grad)
    self_grad = (after(self_grad[0], self_out_grad), self_grad[1])
    gate_grads = lax.all_to_all(
        after(gate_grads, self_grad[0]).reshape(8, own_rows, -1), eight, 0, 0, tiled=True
    )

    def self_attention_back(side, forward, lengths, partial):
        return attention_call(
            self_backward_kernel,
            lengths,
            tables,
            [forward[0], forward[2], self_grad[side]],
            [qkv_full, self_out_full],
            [(2 * span, slab_width, BF)] + [(2 * span, width, BF)] * partial,
            "self_backward",
            10,
        )

    proj_there, back_there = self_attention_back(1, self_there, seq_there, 1)
    (proj_here,) = self_attention_back(0, self_here, seq_here, 0)
    proj_here = after(proj_here, (gate_grads, cross_grads))
    qkv_grads = scatter_z(weight_grad(first, (proj_here, proj_there), own_rows).reshape(-1, slab_width))
    parts, _ = reduce_eight(
        project_last(proj_here, qkv_full, swap(back_there, "c"), hidden_here, ff_full, mlp_there), 2
    )
    d_tokens, block_out, squares_last = rows_call(
        last_rows_kernel,
        [bounds, after_cross, grad_after_self, tokens],
        parts,
        [((rows, width), F32), ((rows, width), BF), ((8, LANES), F32)],
        "last_rows",
        4,
    )
    squares = jnp.concatenate([squares_self[:2], squares_cross[:2], squares_last[:2], squares_last[:2]], axis=0)
    squares = jnp.sum(sum_everywhere(squares), axis=1)[:6]
    rms_stats = jnp.sqrt(squares / (jnp.sum(seq_lengths).astype(F32) * width))

    d_down = after(d_down, proj_here).astype(F32)
    d_gate_up, gain_third = collect_gate(gate_grads, w_gate_up, gains[2], hidden_own)
    d_cross_out = cross_grads[slab_rows:].reshape(own_rows, width)
    out_grads = permute_back(jnp.stack([d_self_out, d_cross_out])).astype(F32)
    cross_grads = lax.all_to_all(cross_grads[:slab_rows].reshape(8, own_rows, -1), eight, 0, 0, tiled=True)
    d_cross_q, d_cross_kv = cross_unslab(cross_grads)
    d_cross_q, gain_second = gained(d_cross_q.astype(F32), w_cross_q, gains[1])
    qkv_grads = lax.all_to_all(qkv_grads.reshape(8, own_rows, -1), eight, 0, 0, tiled=True)
    d_qkv, gain_first = gained(unslab(qkv_grads).astype(F32), w_qkv, gains[0])
    return (
        block_out,
        d_tokens,
        d_conditioning,
        jnp.stack([gain_first, gain_second, gain_third]),
        d_qkv,
        out_grads[0],
        d_cross_q,
        d_cross_kv.astype(F32),
        out_grads[1],
        d_gate_up,
        d_down,
        rms_stats,
    )


def solution(mesh):
    seq_count, fsdp_count = mesh.devices.shape
    fine = Mesh(mesh.devices.reshape(seq_count, fsdp_count // 4, 2, 2), ALL)
    by_token = P(("z", "y", "c", "s"), None)
    by_sequence = P(("z", "y", "c"), None)
    by_row = P(ALL, None)
    by_column = P(None, ALL)
    return jax.shard_map(
        shards,
        mesh=fine,
        in_specs=(by_token, by_sequence, P(), P(), by_column) + (by_row,) * 7 + (by_token,),
        out_specs=(by_token, by_token, by_sequence, by_column) + (by_row,) * 7 + (P(),),
        check_vma=False,
    )
```

```python
import functools
import math

import jax
import jax.numpy as jnp
from jax import lax
from jax.experimental import pallas as pl
from jax.experimental.pallas import tpu as pltpu
from jax.sharding import Mesh, PartitionSpec as P

HD = 64
LANES = 128
BF = jnp.bfloat16
F32 = jnp.float32
ALL = ("s", "z", "y", "c")


def nt(left, right):
    return lax.dot_general(left, right, (((1,), (1,)), ((), ())), preferred_element_type=F32)


def tn(left, right):
    return lax.dot_general(left, right, (((0,), (0,)), ((), ())), preferred_element_type=F32)


def nn(left, right):
    return lax.dot_general(left, right, (((1,), (0,)), ((), ())), preferred_element_type=F32)


def swap(value, axis):
    return lax.ppermute(value, axis, [(0, 1), (1, 0)])


def after(value, earlier):
    return lax.optimization_barrier((value, earlier))[0]


def gather_z(value):
    return lax.all_gather(value, "z", axis=0, tiled=True)


def scatter_z(value):
    return lax.psum_scatter(value, "z", scatter_dimension=0, tiled=True)


def cost(micros):
    return pl.CostEstimate(
        flops=int(1024 + micros * 1e9), transcendentals=0, bytes_accessed=int(1024 + micros * 3e6)
    )


def assemble_kernel(moves, *refs):
    sources, target = refs[:-1], refs[-1]
    for source, start, offset, size in moves:
        target[offset : offset + size] = sources[source][start : start + size]


def assemble(sources, moves, total, micros=0):
    width = sources[0].shape[1]
    column = 384 if width % 384 == 0 else width

    def block(height):
        return pl.BlockSpec((height, column), lambda j: (0, j))

    return pl.pallas_call(
        functools.partial(assemble_kernel, tuple(moves)),
        out_shape=jax.ShapeDtypeStruct((total, width), sources[0].dtype),
        grid=(width // column,),
        in_specs=[block(source.shape[0]) for source in sources],
        out_specs=block(total),
        compiler_params=pltpu.CompilerParams(vmem_limit_bytes=48 << 20),
        cost_estimate=cost(micros),
        name="assemble",
    )(*sources)


def gather_eight(low, high, micros=0, earlier=None):
    half = low.shape[0]
    s_high, y_low = swap(high, "s"), swap(low, "y")
    s_low, y_high = swap(low, "s"), swap(high, "y")
    if earlier is None:
        far_low, far_high = swap(y_low, "s"), swap(s_high, "y")
    else:
        far_low, far_high = swap(after(y_low, earlier), "s"), swap(after(s_high, earlier), "y")
    pieces = [high, s_high, s_low, low, y_low, far_low, far_high, y_high]
    here = assemble(pieces, [(i, 0, i * half, half) for i in range(8)], 8 * half, micros)
    return (here, swap(here, "c")), (y_low, s_high, s_low, y_high)


def half_positions(s_rank, rows):
    half = rows // 2
    step = jnp.arange(half, dtype=jnp.int32)
    mine, across = s_rank * rows + step, (1 - s_rank) * rows + step
    return jnp.stack(
        [
            jnp.concatenate([mine + half, across + half, across, mine]),
            jnp.concatenate([mine, across, across + half, mine + half]),
        ]
    )


def project_kernel(form, merged, value, weight, *refs):
    product = form(value[...], weight[...])
    if not merged:
        refs[0][...] = product.astype(refs[0].dtype)
        return
    product = product + refs[0][...].astype(F32)
    half = refs[1].shape[0]
    for index, block in enumerate((3, 4, 0, 1, 2, 5, 7, 6)):
        out = refs[1 + index]
        out[...] = product[block * half : (block + 1) * half].astype(out.dtype)


def project(value, weight, form, width, received=None, row_block=0, micros=0):
    rows, depth = value.shape
    column = 384
    weight_block = (
        pl.BlockSpec((depth, column), lambda j: (row_block, j))
        if form is nn
        else pl.BlockSpec((column, depth), lambda j: (j, 0))
    )

    def block(height):
        return pl.BlockSpec((height, column), lambda j: (0, j))

    merged = received is not None
    if merged:
        outs = [jax.ShapeDtypeStruct((rows // 8, width), F32 if i < 4 else BF) for i in range(8)]
    else:
        outs = [jax.ShapeDtypeStruct((rows, width), BF)]
    return pl.pallas_call(
        functools.partial(project_kernel, form, merged),
        out_shape=outs,
        grid=(width // column,),
        in_specs=[pl.BlockSpec((rows, depth), lambda j: (0, 0)), weight_block] + [block(rows)] * merged,
        out_specs=[block(o.shape[0]) for o in outs],
        compiler_params=pltpu.CompilerParams(vmem_limit_bytes=48 << 20),
        cost_estimate=cost(micros),
        name="project",
    )(value, weight, *([received] if merged else []))


def add_kernel(left, right, out):
    out[...] = (left[...] + right[...].astype(F32)).astype(BF)


def add_low(left, right, micros=0):
    return pl.pallas_call(
        add_kernel,
        out_shape=jax.ShapeDtypeStruct(left.shape, BF),
        cost_estimate=cost(micros),
        name="add_low",
    )(left, right)


def reduce_eight(blocks, micros=0, earlier=None):
    own_low, y_low, own_high, s_high, to_s, to_s_far, to_y, to_y_far = blocks
    got_far_low, got_far_high = swap(to_s_far, "s"), swap(to_y_far, "y")
    got_low, got_high = swap(to_s, "s"), swap(to_y, "y")
    if earlier is not None:
        got_far_low, got_far_high = after((got_far_low, got_far_high), earlier)
    sum_low, sum_high = add_low(y_low, got_far_low, micros), add_low(s_high, got_far_high, micros)
    parts = (own_low, got_low, swap(sum_low, "y")), (own_high, got_high, swap(sum_high, "s"))
    return parts, (sum_low, sum_high, got_low, got_high)


def sum_everywhere(total):
    for axis in ("c", "y", "s"):
        total = total + swap(total, axis)
    z_count = lax.axis_size("z")
    step = 1
    while step < z_count:
        total = total + lax.ppermute(total, "z", [(i, i ^ step) for i in range(z_count)])
        step *= 2
    return total


def slab(weight):
    rows = weight.shape[0]
    parts = jnp.moveaxis(weight.reshape(rows, 3, 8, -1), 2, 0)
    split = 2 * HD
    return jnp.concatenate(
        [parts[..., :split].reshape(8, rows, -1), parts[..., split:].reshape(8, rows, -1)], axis=-1
    )


def unslab(parts):
    rows = parts.shape[1]
    split = 6 * HD
    merged = jnp.concatenate(
        [parts[..., :split].reshape(8, rows, 3, -1), parts[..., split:].reshape(8, rows, 3, -1)], axis=-1
    )
    return jnp.moveaxis(merged, 0, 2).reshape(rows, -1)


def cross_slab(query, keys_values):
    rows = query.shape[0]
    query = query.reshape(rows, 8, -1)
    keys_values = keys_values.reshape(rows, 2, 8, -1)
    keys, values = keys_values[:, 0], keys_values[:, 1]
    split = 2 * HD
    parts = [keys[..., :split], values[..., :split], keys[..., split:], values[..., split:], query]
    return jnp.moveaxis(jnp.concatenate(parts, axis=-1), 1, 0)


def cross_unslab(parts):
    rows = parts.shape[1]
    parts = jnp.moveaxis(parts, 0, 1)
    keys = jnp.concatenate([parts[..., :128], parts[..., 256:320]], axis=-1)
    values = jnp.concatenate([parts[..., 128:256], parts[..., 320:384]], axis=-1)
    keys_values = jnp.concatenate([keys.reshape(rows, -1), values.reshape(rows, -1)], axis=1)
    return parts[..., 384:].reshape(rows, -1), keys_values


def model_rows(column, rows, width, more=0):
    z_count = lax.axis_size("z")
    stride = column.shape[0] // z_count
    part = 4 * rows
    moves = [
        (0, z * stride + s * part, (s * z_count + z) * part, part) for s in range(2) for z in range(z_count)
    ]
    moves += [(0, z * stride + 2 * part, width + z * more, more) for z in range(z_count) if more]
    return assemble([column], moves, width + z_count * more)


def triples_to_owners(grads, rows):
    count, width = len(grads), grads[0].shape[-1]
    parts = jnp.stack([grad.reshape(-1, 4, rows, width) for grad in grads], axis=2)
    parts = jnp.moveaxis(parts, 1, 0)
    return lax.all_to_all(parts, ("y", "c"), 0, 0, tiled=True).reshape(-1, width)


def gained(grad, weight, gain):
    return grad * gain[:, None], jnp.sum(grad * weight.astype(F32), axis=1)


def head_masks(shape):
    lane = lax.broadcasted_iota(jnp.int32, shape, 1)
    return lane < HD


def rotate(values, cos_ref, down_ref, up_ref, sign):
    ahead = pltpu.roll(values, LANES - 16, 1)
    behind = pltpu.roll(values, 16, 1)
    return values * cos_ref[...] + sign * (ahead * down_ref[...] + behind * up_ref[...])


def forward_heads(query, keys, values, valid):
    left = head_masks(query.shape)
    outs, logs = [], []
    for head in range(2):
        picked = left if head == 0 else jnp.logical_not(left)
        scores = nt(jnp.where(picked, query, jnp.zeros_like(query)), keys) * 0.125
        scores = jnp.where(valid, scores, -1e30)
        peak = jnp.max(scores, axis=-1, keepdims=True)
        expo = jnp.exp(scores - peak)
        total = jnp.sum(expo, axis=-1, keepdims=True)
        probs = (expo * (1.0 / total)).astype(BF)
        outs.append(nn(probs, values))
        logs.append(peak + jnp.log(total))
    return (
        jnp.where(left, outs[0], outs[1]).astype(BF),
        jnp.where(left, logs[0], logs[1]),
    )


def backward_heads(query, keys, values, valid, logsum, grad):
    left = head_masks(query.shape)
    left_keys = head_masks(keys.shape)
    grad_q, grad_k, grad_v = [], [], []
    for head in range(2):
        picked = left if head == 0 else jnp.logical_not(left)
        none = jnp.zeros_like(query)
        scores = nt(jnp.where(picked, query, none), keys) * 0.125
        scores = jnp.where(valid, scores, -1e30)
        probs = jnp.exp(scores - logsum[:, head * HD : head * HD + 1])
        grad_probs = nt(jnp.where(picked, grad, none), values)
        delta = jnp.sum(probs * grad_probs, axis=-1, keepdims=True)
        grad_scores = (probs * (grad_probs - delta)).astype(BF)
        grad_q.append(nn(grad_scores, keys))
        grad_k.append(tn(grad_scores, query))
        grad_v.append(tn(probs.astype(BF), grad))
    return (
        jnp.where(left, grad_q[0], grad_q[1]) * 0.125,
        jnp.where(left_keys, grad_k[0], grad_k[1]) * 0.125,
        jnp.where(left_keys, grad_v[0], grad_v[1]),
    )


def one_head(query, keys, values, valid):
    scores = jnp.where(valid, nt(query, keys) * 0.125, -1e30)
    peak = jnp.max(scores, axis=-1, keepdims=True)
    expo = jnp.exp(scores - peak)
    total = jnp.sum(expo, axis=-1, keepdims=True)
    return nn((expo * (1.0 / total)).astype(BF), values), peak + jnp.log(total)


def one_head_back(query, keys, values, valid, logsum, grad):
    scores = jnp.where(valid, nt(query, keys) * 0.125, -1e30)
    probs = jnp.exp(scores - logsum)
    grad_probs = nt(grad, values)
    delta = jnp.sum(probs * grad_probs, axis=-1, keepdims=True)
    return (probs * (grad_probs - delta)).astype(BF), probs.astype(BF)


def one_head(query, keys, values, valid):
    scores = jnp.where(valid, nt(query, keys) * 0.125, -1e30)
    peak = jnp.max(scores, axis=-1, keepdims=True)
    expo = jnp.exp(scores - peak)
    total = jnp.sum(expo, axis=-1, keepdims=True)
    return nn((expo * (1.0 / total)).astype(BF), values), peak + jnp.log(total)


def one_head_back(query, keys, values, valid, logsum, grad):
    scores = jnp.where(valid, nt(query, keys) * 0.125, -1e30)
    probs = jnp.exp(scores - logsum)
    grad_probs = nt(grad, values)
    delta = jnp.sum(probs * grad_probs, axis=-1, keepdims=True)
    return (probs * (grad_probs - delta)).astype(BF), probs.astype(BF)


def self_forward_kernel(
    lengths, position, cosine, down, up, rows, weight, rotated, mixed, logsum
):
    projected = nn(rows[...], weight[...])
    pieces = [rotate(projected[:, i : i + LANES], cosine, down, up, 1.0).astype(BF) for i in (0, 128, 384)]
    values = projected[:, 256:384].astype(BF)
    values_last = projected[:, 512:576].astype(BF)
    rotated[:, 0:128] = pieces[0]
    rotated[:, 128:256] = pieces[1]
    rotated[:, 256:384] = values
    rotated[:, 384:512] = pieces[2]
    rotated[:, 512:576] = values_last
    valid = position[0:1, :] < lengths[pl.program_id(0)]
    mixed_pair, logsum_pair = forward_heads(pieces[0], pieces[1], values, valid)
    mixed[:, 0:128] = mixed_pair
    logsum[:, 0:128] = logsum_pair
    last = pieces[2]
    left = head_masks(last.shape)
    mixed_last, logsum_last = one_head(
        jnp.where(left, last, jnp.zeros_like(last)), pltpu.roll(last, HD, 1), values_last, valid
    )
    mixed[:, 128:192] = mixed_last.astype(BF)
    logsum[:, 128:192] = jnp.broadcast_to(logsum_last, mixed_last.shape)


def self_backward_kernel(
    lengths, position, cosine, down, up, rotated, logsum, grad_rows, weight, out_weight, grad_out, *partial
):
    grad = nt(grad_rows[...], out_weight[...]).astype(BF)
    valid = position[0:1, :] < lengths[pl.program_id(0)]
    back_q, back_k, back_v = backward_heads(
        rotated[:, 0:128], rotated[:, 128:256], rotated[:, 256:384], valid, logsum[:, 0:128], grad[:, 0:128]
    )
    grad_out[:, 0:128] = rotate(back_q, cosine, down, up, -1.0).astype(BF)
    grad_out[:, 128:256] = rotate(back_k, cosine, down, up, -1.0).astype(BF)
    grad_out[:, 256:384] = back_v.astype(BF)
    last = rotated[:, 384:512]
    turned = pltpu.roll(last, HD, 1)
    left = head_masks(last.shape)
    grad_last = grad[:, 128:192]
    grad_scores, probs = one_head_back(
        jnp.where(left, last, jnp.zeros_like(last)),
        turned,
        rotated[:, 512:576],
        valid,
        logsum[:, 128:129],
        grad_last,
    )
    both = jnp.where(left, nn(grad_scores, turned), pltpu.roll(tn(grad_scores, last), HD, 1)) * 0.125
    grad_out[:, 384:512] = rotate(both, cosine, down, up, -1.0).astype(BF)
    grad_out[:, 512:576] = tn(probs, grad_last).astype(BF)
    for out in partial:
        out[...] = nt(grad_out[...], weight[...]).astype(BF)


def cross_forward_kernel(
    lengths, position, rows, keys_values, weight, query, mixed, logsum
):
    query[...] = nn(rows[...], weight[...]).astype(BF)
    valid = position[0:1, :] < lengths[pl.program_id(0)]
    mixed_pair, logsum_pair = forward_heads(
        query[:, 0:128], keys_values[:, 0:128], keys_values[:, 128:256], valid
    )
    mixed[:, 0:128] = mixed_pair
    logsum[:, 0:128] = logsum_pair
    last = keys_values[:, 256:384]
    values = pltpu.roll(last, HD, 1)[:, 0:HD]
    mixed_last, logsum_last = one_head(query[:, 128:192], last[:, 0:HD], values, valid)
    mixed[:, 128:192] = mixed_last.astype(BF)
    logsum[:, 128:192] = jnp.broadcast_to(logsum_last, mixed_last.shape)


def cross_backward_kernel(
    lengths, position, query, keys_values, logsum, grad_rows, weight, out_weight, grad_q, grad_kv, *partial
):
    grad = nt(grad_rows[...], out_weight[...]).astype(BF)
    valid = position[0:1, :] < lengths[pl.program_id(0)]
    back_q, back_k, back_v = backward_heads(
        query[:, 0:128], keys_values[:, 0:128], keys_values[:, 128:256], valid, logsum[:, 0:128], grad[:, 0:128]
    )
    grad_q[:, 0:128] = back_q.astype(BF)
    grad_kv[:, 0:128] = back_k.astype(BF)
    grad_kv[:, 128:256] = back_v.astype(BF)
    last = keys_values[:, 256:384]
    keys = last[:, 0:HD]
    query_last, grad_last = query[:, 128:192], grad[:, 128:192]
    grad_scores, probs = one_head_back(
        query_last, keys, pltpu.roll(last, HD, 1)[:, 0:HD], valid, logsum[:, 128:129], grad_last
    )
    grad_q[:, 128:192] = (nn(grad_scores, keys) * 0.125).astype(BF)
    grad_kv[:, 256:384] = jnp.concatenate(
        [tn(grad_scores, query_last) * 0.125, tn(probs, grad_last)], axis=1
    ).astype(BF)
    for out in partial:
        out[...] = nt(grad_q[...], weight[...]).astype(BF)


def attention_call(kernel, lengths, tables, inputs, weights, outputs, name, micros=0):
    sequences = lengths.shape[0]

    def block(rows, width):
        return pl.BlockSpec((rows // sequences, width), lambda b, ln: (b, 0))

    def table(value):
        return pl.BlockSpec((None,) + value.shape[1:], lambda b, ln: (b, 0, 0))

    def whole(value):
        return pl.BlockSpec(value.shape, lambda b, ln: (0, 0))

    return pl.pallas_call(
        kernel,
        out_shape=[jax.ShapeDtypeStruct((r, w), dt) for r, w, dt in outputs],
        grid_spec=pltpu.PrefetchScalarGridSpec(
            num_scalar_prefetch=1,
            grid=(sequences,),
            in_specs=[table(t) for t in tables]
            + [block(*i.shape) for i in inputs]
            + [whole(w) for w in weights],
            out_specs=[block(r, w) for r, w, _ in outputs],
        ),
        compiler_params=pltpu.CompilerParams(
            dimension_semantics=("arbitrary",), vmem_limit_bytes=48 << 20
        ),
        cost_estimate=cost(micros),
        name=name,
    )(lengths, *tables, *inputs, *weights)


def feed_forward_kernel(rows, grad_rows, weights, hidden, grad_out, *partial):
    units, width = hidden.shape[1], rows.shape[1]
    gate = nn(rows[...], weights[:width, :units])
    upper = nn(rows[...], weights[:width, units:])
    sig = jax.nn.sigmoid(gate)
    silu = gate * sig
    hidden[...] = (silu * upper).astype(BF)
    grad_hidden = nt(grad_rows[...], weights[width:])
    grad_out[:, :units] = (grad_hidden * upper * (sig * (1.0 + gate * (1.0 - sig)))).astype(BF)
    grad_out[:, units:] = (grad_hidden * silu).astype(BF)
    for out in partial:
        out[...] = nt(grad_out[...], weights[:width]).astype(BF)


def feed_forward(rows, grad_rows, weights, partial):
    total, width = rows.shape
    units = weights.shape[1] // 2
    block = total // 2

    def whole(value):
        return pl.BlockSpec(value.shape, lambda i: (0, 0))

    widths = [units, 2 * units] + [width] * partial
    return pl.pallas_call(
        feed_forward_kernel,
        out_shape=[jax.ShapeDtypeStruct((total, w), BF) for w in widths],
        grid=(2,),
        in_specs=[pl.BlockSpec((block, width), lambda i: (i, 0))] * 2 + [whole(weights)],
        out_specs=[pl.BlockSpec((block, w), lambda i: (i, 0)) for w in widths],
        compiler_params=pltpu.CompilerParams(vmem_limit_bytes=56 << 20),
        cost_estimate=cost(10),
        name="feed_forward",
    )(rows, grad_rows, weights)


def weight_grad_kernel(here, there, grad_here, grad_there, out):
    grad = tn(here[...], grad_here[...]) + tn(there[...], grad_there[...])
    out[...] = grad.astype(BF).reshape(out.shape)


def weight_grad(rows, grads, own_rows=None):
    total, width = rows[0].shape
    columns = grads[0].shape[1]
    block = 3 * LANES
    steps = width // block
    if own_rows is None:
        out_shape, out_block = (width, columns), pl.BlockSpec((block, columns), lambda i: (i, 0))
    else:
        z_count, part = lax.axis_size("z"), 4 * own_rows
        turn = steps // 2
        out_shape = (z_count, 2, part, columns)
        out_block = pl.BlockSpec((block // part, None, part, columns), lambda i: (i % turn, i // turn, 0, 0))
    return pl.pallas_call(
        weight_grad_kernel,
        out_shape=jax.ShapeDtypeStruct(out_shape, BF),
        grid=(steps,),
        in_specs=[pl.BlockSpec((total, block), lambda i: (0, i))] * 2
        + [pl.BlockSpec((total, columns), lambda i: (0, 0))] * 2,
        out_specs=out_block,
        compiler_params=pltpu.CompilerParams(vmem_limit_bytes=48 << 20),
        cost_estimate=cost(total * width * columns / 2e8),
        name="weight_grad",
    )(*rows, *grads)


def spread_gate_kernel(unit, gain, weight, out):
    scaled = weight[...].astype(F32) * gain[...]
    corners, _, width = out.shape
    for z in range(width // unit):
        for corner in range(corners):
            start = (z * corners + corner) * unit
            out[corner, :, z * unit : (z + 1) * unit] = scaled[:, start : start + unit].astype(BF)


def spread_gate(weight, gain, unit):
    rows, columns = weight.shape
    quarter = columns // 4
    return pl.pallas_call(
        functools.partial(spread_gate_kernel, unit),
        out_shape=jax.ShapeDtypeStruct((8, rows, columns // 8), BF),
        grid=(2, 2),
        in_specs=[
            pl.BlockSpec((rows, 1), lambda g, s: (0, 0)),
            pl.BlockSpec((rows, quarter), lambda g, s: (0, 2 * g + s)),
        ],
        out_specs=pl.BlockSpec((4, rows, quarter // 4), lambda g, s: (s, 0, g)),
        cost_estimate=cost(0),
        name="spread_gate",
    )(gain[:, None], weight)


def collect_gate_kernel(unit, gain, weight, grads, out, sums):
    @pl.when((pl.program_id(0) == 0) & (pl.program_id(1) == 0))
    def _():
        sums[...] = jnp.zeros_like(sums)

    corners, rows, width = grads.shape
    total = jnp.zeros((rows, 1), F32)
    for z in range(width // unit):
        for corner in range(corners):
            cut = slice((z * corners + corner) * unit, (z * corners + corner + 1) * unit)
            grad = grads[corner, :, z * unit : (z + 1) * unit].astype(F32)
            out[:, cut] = grad * gain[...]
            total = total + jnp.sum(grad * weight[:, cut].astype(F32), axis=1, keepdims=True)
    sums[...] = sums[...] + total


def collect_gate(grads, weight, gain, unit):
    rows, columns = weight.shape
    quarter = columns // 4
    grad, sums = pl.pallas_call(
        functools.partial(collect_gate_kernel, unit),
        out_shape=[jax.ShapeDtypeStruct((rows, columns), F32), jax.ShapeDtypeStruct((rows, LANES), F32)],
        grid=(2, 2),
        in_specs=[
            pl.BlockSpec((rows, 1), lambda g, s: (0, 0)),
            pl.BlockSpec((rows, quarter), lambda g, s: (0, 2 * g + s)),
            pl.BlockSpec((4, rows, quarter // 4), lambda g, s: (s, 0, g)),
        ],
        out_specs=[
            pl.BlockSpec((rows, quarter), lambda g, s: (0, 2 * g + s)),
            pl.BlockSpec((rows, LANES), lambda g, s: (0, 0)),
        ],
        cost_estimate=cost(10),
        name="collect_gate",
    )(gain[:, None], weight, grads)
    return grad, sums[:, 0]


def normalize(hidden):
    centred = hidden - jnp.mean(hidden, axis=-1, keepdims=True)
    inverse = lax.rsqrt(jnp.mean(centred * centred, axis=-1, keepdims=True) + 1e-05)
    return centred * inverse, inverse


def layer_norm_back(hidden, scaled):
    unit, inverse = normalize(hidden)
    return inverse * (
        scaled
        - jnp.mean(scaled, axis=-1, keepdims=True)
        - unit * jnp.mean(scaled * unit, axis=-1, keepdims=True)
    )


def total_of(parts):
    return parts[0][...] + parts[1][...].astype(F32) + parts[2][...].astype(F32)


def lane_sums(value):
    sums = jnp.sum(value, axis=0, keepdims=True)
    return sum(sums[:, i : i + LANES] for i in range(0, sums.shape[1], LANES))


def forward_rows_kernel(bounds, stream, *refs):
    parts, (stream_out, low_out, high_out, squares) = (refs[:3], refs[3:6]), refs[6:]
    half = low_out.shape[0]
    sums = [0.0, 0.0]
    for index, out in enumerate((low_out, high_out)):
        rows = slice(index * half, (index + 1) * half)
        branch = total_of(parts[index])
        hidden = stream[rows] + branch
        stream_out[rows] = hidden
        out[...] = normalize(hidden)[0].astype(BF)
        position = bounds[0] + index * half + lax.broadcasted_iota(jnp.int32, (half, 1), 0)
        weight = jnp.where(position < bounds[1], 1.0, 0.0)
        sums = [sums[0] + lane_sums(branch * branch * weight), sums[1] + lane_sums(hidden * hidden * weight)]
    squares[0:1] = sums[0]
    squares[1:2] = sums[1]


def last_rows_kernel(bounds, stream, *refs):
    parts, (stream_out, squares) = (refs[:3], refs[3:6]), refs[6:]
    half = parts[0][0].shape[0]
    sums = [0.0, 0.0]
    for index in range(2):
        rows = slice(index * half, (index + 1) * half)
        branch = total_of(parts[index])
        hidden = stream[rows] + branch
        stream_out[rows] = hidden.astype(BF)
        position = bounds[0] + index * half + lax.broadcasted_iota(jnp.int32, (half, 1), 0)
        weight = jnp.where(position < bounds[1], 1.0, 0.0)
        sums = [sums[0] + lane_sums(branch * branch * weight), sums[1] + lane_sums(hidden * hidden * weight)]
    squares[0:1] = sums[0]
    squares[1:2] = sums[1]


def backward_rows_kernel(grad, stream, *refs):
    parts, outs = (refs[:3], refs[3:6]), refs[6:]
    half = parts[0][0].shape[0]
    for index in range(2):
        rows = slice(index * half, (index + 1) * half)
        total = grad[rows].astype(F32) + layer_norm_back(stream[rows].astype(F32), total_of(parts[index]))
        outs[0][rows] = total
        if len(outs) > 1:
            outs[1 + index][...] = total.astype(BF)


def rows_call(kernel, leading, parts, outputs, name, micros=0):
    vmem = pl.BlockSpec(memory_space=pltpu.VMEM)
    smem = pl.BlockSpec(memory_space=pltpu.SMEM)
    operands = list(leading) + list(parts[0]) + list(parts[1])
    return pl.pallas_call(
        kernel,
        out_shape=[jax.ShapeDtypeStruct(shape, dt) for shape, dt in outputs],
        in_specs=[smem if o.ndim == 1 else vmem for o in operands],
        out_specs=[vmem] * len(outputs),
        compiler_params=pltpu.CompilerParams(vmem_limit_bytes=48 << 20),
        cost_estimate=cost(micros),
        name=name,
    )(*operands)


def shards(
    tokens,
    conditioning,
    seq_lengths,
    cond_lengths,
    norm_gains,
    w_qkv,
    w_self_out,
    w_cross_q,
    w_cross_kv,
    w_cross_out,
    w_gate_up,
    w_down,
    out_grad,
):
    rows, width = tokens.shape
    half = rows // 2
    z_count = lax.axis_size("z")
    own_rows = w_qkv.shape[0]
    hidden_own = w_down.shape[0]
    s_rank, z_rank = lax.axis_index("s"), lax.axis_index("z")
    y_rank, c_rank = lax.axis_index("y"), lax.axis_index("c")
    span = 2 * rows

    first_seq = (z_rank * 2 + y_rank) * 2
    mine, other = first_seq + c_rank, first_seq + 1 - c_rank
    across, corner = (z_rank * 2 + 1 - y_rank) * 2 + c_rank, (z_rank * 2 + 1 - y_rank) * 2 + 1 - c_rank
    seq_here = jnp.stack([seq_lengths[mine], seq_lengths[across]])
    seq_there = jnp.stack([seq_lengths[other], seq_lengths[corner]])
    cond_here_lengths = jnp.stack([cond_lengths[mine], cond_lengths[across]])
    cond_there_lengths = jnp.stack([cond_lengths[other], cond_lengths[corner]])
    bounds = jnp.stack([s_rank * rows, seq_lengths[mine]])
    positions = half_positions(s_rank, rows)
    lane = jnp.arange(LANES, dtype=jnp.int32) % HD
    freqs = jnp.exp((lane % 16).astype(F32) * (-math.log(10000.0) / 16.0))
    angles = positions.astype(F32)[..., None] * freqs
    cosine = jnp.where(lane < 32, jnp.cos(angles), 1.0)
    sine = jnp.sin(angles)
    down = jnp.where(lane < 16, -sine, 0.0)
    up = jnp.where((lane >= 16) & (lane < 32), sine, 0.0)
    tables = [jnp.broadcast_to(positions[:, None, :], (2, 8, span)), cosine, down, up]
    cond_rows = conditioning.shape[0]
    cond_position = jnp.broadcast_to(jnp.arange(cond_rows, dtype=jnp.int32), (2, 8, cond_rows))

    eight = ("s", "y", "c")
    gains = norm_gains.astype(F32)
    qkv_parts = slab((w_qkv.astype(F32) * gains[0][:, None]).astype(BF))
    qkv_parts = lax.all_to_all(qkv_parts, eight, 0, 0, tiled=True)
    slab_width = qkv_parts.shape[-1]
    head_width = slab_width // 3
    slab_rows = 8 * own_rows

    def out_rows(column):
        column = column.reshape(z_count, -1, slab_width)[:, slab_rows:].reshape(4, -1, own_rows, width)
        column = lax.all_to_all(column, ("y", "c"), 0, 0, tiled=True)
        return jnp.moveaxis(column, 0, 1).reshape(-1, width)

    qkv_both = jnp.concatenate([qkv_parts.reshape(slab_rows, -1), w_self_out.reshape(-1, slab_width)], axis=0)
    qkv_column = gather_z(qkv_both)
    first_unit = normalize(tokens.astype(F32))[0].astype(BF)
    first, arrived = gather_eight(first_unit[:half], first_unit[half:])
    conditioning, cross_q_own, cross_kv_own = after((conditioning, w_cross_q, w_cross_kv), (first[0], qkv_both))
    cond_here = jnp.concatenate([conditioning, swap(conditioning, "y")], axis=0)
    cond = (cond_here, swap(cond_here, "c"))
    cross_parts = cross_slab((cross_q_own.astype(F32) * gains[1][:, None]).astype(BF), cross_kv_own)
    cross_parts = lax.all_to_all(cross_parts, eight, 0, 0, tiled=True)
    cross_both = jnp.concatenate([cross_parts.reshape(slab_rows, -1), w_cross_out.reshape(-1, slab_width)], axis=0)
    cross_column = gather_z(cross_both)
    gate_parts = spread_gate(after(w_gate_up, first[0]), gains[2], hidden_own)
    gate_parts = lax.all_to_all(after(gate_parts, (cross_both, cond_here)), eight, 0, 0, tiled=True)
    qkv_column = after(qkv_column, cond_here)
    qkv_full = model_rows(qkv_column, own_rows, width)

    def self_attention(side, lengths):
        return attention_call(
            self_forward_kernel,
            lengths,
            tables,
            [first[side]],
            [qkv_full],
            [(2 * span, slab_width, BF), (2 * span, head_width, BF), (2 * span, head_width, F32)],
            "self_forward",
            7,
        )

    out_grads_all, arrived = gather_eight(*after((out_grad[:half], out_grad[half:]), qkv_full))
    self_here = self_attention(0, seq_here)
    self_out_full = out_rows(after(qkv_column, self_here[1]))
    self_there = self_attention(1, seq_there)
    ff_column = gather_z(after(jnp.concatenate([gate_parts.reshape(slab_rows, -1), w_down], axis=0), self_here[1]))
    (self_partial,) = project(after(self_there[1], (arrived, out_grads_all[0])), self_out_full, nn, width)
    parts, sent = reduce_eight(project(self_here[1], self_out_full, nn, width, swap(self_partial, "c")))
    forward_outs = [((rows, width), F32), ((half, width), BF), ((half, width), BF), ((8, LANES), F32)]
    cross_column = after(cross_column, sent)
    cross_full = model_rows(cross_column, own_rows, width)
    kv_width = 2 * head_width
    cross_kv_full, cross_q_full = cross_full[:, :kv_width], cross_full[:, kv_width:]
    cond_proj = [nn(c, cross_kv_full).astype(BF) for c in cond]
    parts = after(parts, (cond_proj, cross_q_full))
    after_self, second_low, second_high, squares_self = rows_call(
        forward_rows_kernel, [bounds, tokens.astype(F32)], parts, forward_outs, "forward_rows"
    )

    second, arrived = gather_eight(second_low, second_high)
    cross_out_full = out_rows(after(cross_column, arrived))

    def cross_attention(side, lengths):
        return attention_call(
            cross_forward_kernel,
            lengths,
            [cond_position],
            [second[side], cond_proj[side]],
            [cross_q_full],
            [(2 * span, head_width, BF), (2 * span, head_width, BF), (2 * span, head_width, F32)],
            "cross_forward",
        )

    cross_here = cross_attention(0, cond_here_lengths)
    cross_there = cross_attention(1, cond_there_lengths)
    (cross_partial,) = project(cross_there[1], cross_out_full, nn, width)
    parts, sent = reduce_eight(project(cross_here[1], cross_out_full, nn, width, swap(cross_partial, "c")))
    ff_full = model_rows(after(ff_column, sent), own_rows, width, hidden_own)
    parts = after(parts, ff_full)
    after_cross, third_low, third_high, squares_cross = rows_call(
        forward_rows_kernel, [bounds, after_self], parts, forward_outs, "forward_rows"
    )

    third, _ = gather_eight(third_low, third_high)
    hidden_there, gates_there, back_there = feed_forward(third[1], out_grads_all[1], ff_full, 1)
    hidden_here, gates_here = feed_forward(third[0], out_grads_all[0], ff_full, 0)
    parts, sent = reduce_eight(project(gates_here, ff_full, nt, width, swap(back_there, "c"), micros=8), 2)
    hidden_here, hidden_there, gates_here, gates_there = after(
        (hidden_here, hidden_there, gates_here, gates_there), sent
    )
    down_grad = weight_grad((hidden_here, hidden_there), out_grads_all)
    d_down = scatter_z(down_grad)
    parts = after(parts, down_grad)
    backward_outs = [((rows, width), F32), ((half, width), BF), ((half, width), BF)]
    grad_after_cross, cross_low, cross_high = rows_call(
        backward_rows_kernel, [out_grad, after_cross], parts, backward_outs, "backward_rows", 3
    )

    cross_grad, sent = gather_eight(cross_low, cross_high, 3)
    gate_grad = weight_grad(third, after((gates_here, gates_there), sent), own_rows)
    gate_grads = scatter_z(after(gate_grad, d_down).reshape(-1, gate_grad.shape[-1]))
    cross_grad = after(cross_grad, gate_grad)

    def cross_attention_back(side, forward, lengths, partial):
        return attention_call(
            cross_backward_kernel,
            lengths,
            [cond_position],
            [forward[0], cond_proj[side], forward[2], cross_grad[side]],
            [cross_q_full, cross_out_full],
            [(2 * span, head_width, BF), (2 * cond_rows, kv_width, BF)] + [(2 * span, width, BF)] * partial,
            "cross_backward",
            5,
        )

    back_there = cross_attention_back(1, cross_there, cond_there_lengths, 1)
    back_here = cross_attention_back(0, cross_here, cond_here_lengths, 0)
    parts, sent = reduce_eight(
        project(back_here[0], cross_q_full, nt, width, swap(back_there[2], "c"), micros=5), 2
    )
    back_queries, back_keys = after(((back_here[0], back_there[0]), (back_here[1], back_there[1])), sent)
    cross_grads = jnp.concatenate(
        [weight_grad(cond, back_keys, own_rows), weight_grad(second, back_queries, own_rows)], axis=-1
    )
    cross_out_grad = (tn(cross_here[1], cross_grad[0]) + tn(cross_there[1], cross_grad[1])).astype(BF)
    parts = after(parts, (cross_grads, cross_out_grad, d_down))
    grad_after_self, self_low, self_high = rows_call(
        backward_rows_kernel, [grad_after_cross, after_self], parts, backward_outs, "backward_rows", 3
    )

    self_grad, sent = gather_eight(self_low, self_high, 3)
    down_block = width // hidden_here.shape[1]
    (mlp_there,) = project(after(hidden_there, sent), ff_full, nn, width, None, down_block, 5)
    mlp_blocks = project(hidden_here, ff_full, nn, width, swap(mlp_there, "c"), down_block, 5)
    mlp_blocks = after(mlp_blocks, self_grad[0])
    self_out_grad = (tn(self_here[1], self_grad[0]) + tn(self_there[1], self_grad[1])).astype(BF)
    out_grads = triples_to_owners((self_out_grad, cross_out_grad), own_rows)
    cross_grads = scatter_z(after(cross_grads, (gate_grads, self_grad[0])).reshape(-1, slab_width))
    out_grads = scatter_z(after(out_grads, cross_grads))
    self_grad = (after(self_grad[0], self_out_grad), self_grad[1])
    gate_grads = lax.all_to_all(
        after(gate_grads, self_grad[0]).reshape(8, own_rows, -1), eight, 0, 0, tiled=True
    )

    def self_attention_back(side, forward, lengths, partial):
        return attention_call(
            self_backward_kernel,
            lengths,
            tables,
            [forward[0], forward[2], self_grad[side]],
            [qkv_full, self_out_full],
            [(2 * span, slab_width, BF)] + [(2 * span, width, BF)] * partial,
            "self_backward",
            10,
        )

    key_here, key_there = after(back_keys, self_grad[0])
    cond_there = swap(nt(key_there, cross_kv_full).astype(BF), "c")
    proj_there, back_there = self_attention_back(1, self_there, seq_there, 1)
    cond_back = nt(key_here, cross_kv_full) + after(cond_there, proj_there).astype(F32)
    cond_across = swap(cond_back[cond_rows:].astype(BF), "y")
    mlp_parts, sent = reduce_eight(mlp_blocks, 2, proj_there)
    self_grad = (after(self_grad[0], sent), self_grad[1])
    (proj_here,) = self_attention_back(0, self_here, seq_here, 0)
    cond_back = cond_back[:cond_rows] + after(cond_across, proj_here).astype(F32)
    d_conditioning = cond_back.astype(BF).astype(F32) + swap(cond_back.astype(BF), "s").astype(F32)
    proj_here = after(proj_here, (gate_grads, cross_grads))
    qkv_grads = weight_grad(first, (proj_here, proj_there), own_rows)
    qkv_grads = scatter_z(after(qkv_grads, out_grads).reshape(-1, slab_width))
    blocks = project(after(proj_here, out_grads), qkv_full, nt, width, swap(back_there, "c"), micros=5)
    parts, sent = reduce_eight(blocks, 2)
    mlp_parts = after(mlp_parts, blocks)
    block_out, squares_last = rows_call(
        last_rows_kernel,
        [bounds, after_cross],
        mlp_parts,
        [((rows, width), BF), ((8, LANES), F32)],
        "last_rows",
        3,
    )
    (d_tokens,) = rows_call(
        backward_rows_kernel,
        [grad_after_self, tokens],
        parts,
        backward_outs[:1],
        "backward_rows",
        3,
    )
    squares = jnp.concatenate([squares_self[:2], squares_cross[:2], squares_last[:2], squares_last[:2]], axis=0)
    squares = sum_everywhere(squares)
    qkv_grads = after(qkv_grads, squares).reshape(8, own_rows, -1)
    qkv_parts = lax.all_to_all(qkv_grads, eight, 0, 0, tiled=True)
    squares = jnp.sum(squares, axis=1)[:6]
    rms_stats = jnp.sqrt(squares / (jnp.sum(seq_lengths).astype(F32) * width))


    d_down = after(d_down, proj_here).astype(F32)
    gate_grads = after(gate_grads, squares_last)
    d_gate_up, gain_third = collect_gate(gate_grads, w_gate_up, gains[2], hidden_own)
    cross_grads = lax.all_to_all(cross_grads.reshape(8, own_rows, -1), eight, 0, 0, tiled=True)
    d_cross_q, d_cross_kv = cross_unslab(cross_grads)
    d_cross_q, gain_second = gained(d_cross_q.astype(F32), w_cross_q, gains[1])
    d_qkv, gain_first = gained(unslab(qkv_parts).astype(F32), w_qkv, gains[0])
    return (
        block_out,
        d_tokens,
        d_conditioning,
        jnp.stack([gain_first, gain_second, gain_third]),
        d_qkv,
        out_grads[:own_rows].astype(F32),
        d_cross_q,
        d_cross_kv.astype(F32),
        out_grads[own_rows:].astype(F32),
        d_gate_up,
        d_down,
        rms_stats,
    )


def solution(mesh):
    seq_count, fsdp_count = mesh.devices.shape
    fine = Mesh(mesh.devices.reshape(seq_count, fsdp_count // 4, 2, 2), ALL)
    by_token = P(("z", "y", "c", "s"), None)
    by_sequence = P(("z", "y", "c"), None)
    by_row = P(ALL, None)
    by_column = P(None, ALL)
    return jax.shard_map(
        shards,
        mesh=fine,
        in_specs=(by_token, by_sequence, P(), P(), by_column) + (by_row,) * 7 + (by_token,),
        out_specs=(by_token, by_token, by_sequence, by_column) + (by_row,) * 7 + (P(),),
        check_vma=False,
    )
```

```python
import functools
import math

import jax
import jax.numpy as jnp
from jax import lax
from jax.experimental import pallas as pl
from jax.experimental.pallas import tpu as pltpu
from jax.sharding import Mesh, PartitionSpec as P

HD = 64
LANES = 128
BF = jnp.bfloat16
F32 = jnp.float32
ALL = ("s", "z", "y", "c")


def nt(left, right):
    return lax.dot_general(left, right, (((1,), (1,)), ((), ())), preferred_element_type=F32)


def tn(left, right):
    return lax.dot_general(left, right, (((0,), (0,)), ((), ())), preferred_element_type=F32)


def nn(left, right):
    return lax.dot_general(left, right, (((1,), (0,)), ((), ())), preferred_element_type=F32)


def swap(value, axis):
    return lax.ppermute(value, axis, [(0, 1), (1, 0)])


def after(value, earlier):
    return lax.optimization_barrier((value, earlier))[0]


def gather_z(value):
    return lax.all_gather(value, "z", axis=0, tiled=True)


def scatter_z(value):
    return lax.psum_scatter(value, "z", scatter_dimension=0, tiled=True)


def cost(micros):
    return pl.CostEstimate(
        flops=int(1024 + micros * 1e9), transcendentals=0, bytes_accessed=int(1024 + micros * 3e6)
    )


def assemble_kernel(moves, *refs):
    sources, target = refs[:-1], refs[-1]
    for source, start, offset, size in moves:
        target[offset : offset + size] = sources[source][start : start + size]


def assemble(sources, moves, total, micros=0):
    width = sources[0].shape[1]
    column = 384 if width % 384 == 0 else width

    def block(height):
        return pl.BlockSpec((height, column), lambda j: (0, j))

    return pl.pallas_call(
        functools.partial(assemble_kernel, tuple(moves)),
        out_shape=jax.ShapeDtypeStruct((total, width), sources[0].dtype),
        grid=(width // column,),
        in_specs=[block(source.shape[0]) for source in sources],
        out_specs=block(total),
        compiler_params=pltpu.CompilerParams(vmem_limit_bytes=48 << 20),
        cost_estimate=cost(micros),
        name="assemble",
    )(*sources)


def gather_eight(low, high, micros=0, beside=None):
    half = low.shape[0]
    s_high, y_low = swap(high, "s"), swap(low, "y")
    s_low, y_high = swap(low, "s"), swap(high, "y")
    far_low, far_high = swap(y_low, "s"), swap(s_high, "y")
    if beside is not None:
        beside = beside((y_low, s_high))
        far_low, far_high = after((far_low, far_high), beside)
    pieces = [high, s_high, s_low, low, y_low, far_low, far_high, y_high]
    here = assemble(pieces, [(i, 0, i * half, half) for i in range(8)], 8 * half, micros)
    return (here, swap(here, "c")), (y_low, s_high) if beside is None else beside


def half_positions(s_rank, rows):
    half = rows // 2
    step = jnp.arange(half, dtype=jnp.int32)
    mine, across = s_rank * rows + step, (1 - s_rank) * rows + step
    return jnp.stack(
        [
            jnp.concatenate([mine + half, across + half, across, mine]),
            jnp.concatenate([mine, across, across + half, mine + half]),
        ]
    )


def project_kernel(form, merged, value, weight, *refs):
    product = form(value[...], weight[...])
    if not merged:
        refs[0][...] = product.astype(refs[0].dtype)
        return
    product = product + refs[0][...].astype(F32)
    half = refs[1].shape[0]
    for index, block in enumerate((3, 4, 0, 1, 2, 5, 7, 6)):
        out = refs[1 + index]
        out[...] = product[block * half : (block + 1) * half].astype(out.dtype)


def project(value, weight, form, width, received=None, row_block=0, micros=0):
    rows, depth = value.shape
    column = 384
    weight_block = (
        pl.BlockSpec((depth, column), lambda j: (row_block, j))
        if form is nn
        else pl.BlockSpec((column, depth), lambda j: (j, 0))
    )

    def block(height):
        return pl.BlockSpec((height, column), lambda j: (0, j))

    merged = received is not None
    if merged:
        outs = [jax.ShapeDtypeStruct((rows // 8, width), F32 if i < 4 else BF) for i in range(8)]
    else:
        outs = [jax.ShapeDtypeStruct((rows, width), BF)]
    return pl.pallas_call(
        functools.partial(project_kernel, form, merged),
        out_shape=outs,
        grid=(width // column,),
        in_specs=[pl.BlockSpec((rows, depth), lambda j: (0, 0)), weight_block] + [block(rows)] * merged,
        out_specs=[block(o.shape[0]) for o in outs],
        compiler_params=pltpu.CompilerParams(vmem_limit_bytes=48 << 20),
        cost_estimate=cost(micros),
        name="project",
    )(value, weight, *([received] if merged else []))


def add_kernel(left, right, out):
    out[...] = (left[...] + right[...].astype(F32)).astype(BF)


def add_low(left, right, micros=0):
    return pl.pallas_call(
        add_kernel,
        out_shape=jax.ShapeDtypeStruct(left.shape, BF),
        cost_estimate=cost(micros),
        name="add_low",
    )(left, right)


def reduce_eight(blocks, micros=0, earlier=None):
    own_low, y_low, own_high, s_high, to_s, to_s_far, to_y, to_y_far = blocks
    got_far_low, got_far_high = swap(to_s_far, "s"), swap(to_y_far, "y")
    got_low, got_high = swap(to_s, "s"), swap(to_y, "y")
    if earlier is not None:
        got_far_low, got_far_high = after((got_far_low, got_far_high), earlier)
    sum_low, sum_high = add_low(y_low, got_far_low, micros), add_low(s_high, got_far_high, micros)
    parts = (own_low, got_low, swap(sum_low, "y")), (own_high, got_high, swap(sum_high, "s"))
    return parts, (sum_low, sum_high, got_low, got_high)


def sum_everywhere(total):
    for axis in ("c", "y", "s"):
        total = total + swap(total, axis)
    z_count = lax.axis_size("z")
    step = 1
    while step < z_count:
        total = total + lax.ppermute(total, "z", [(i, i ^ step) for i in range(z_count)])
        step *= 2
    return total


def slab(weight):
    rows = weight.shape[0]
    parts = jnp.moveaxis(weight.reshape(rows, 3, 8, -1), 2, 0)
    split = 2 * HD
    return jnp.concatenate(
        [parts[..., :split].reshape(8, rows, -1), parts[..., split:].reshape(8, rows, -1)], axis=-1
    )


def unslab(parts):
    rows = parts.shape[1]
    split = 6 * HD
    merged = jnp.concatenate(
        [parts[..., :split].reshape(8, rows, 3, -1), parts[..., split:].reshape(8, rows, 3, -1)], axis=-1
    )
    return jnp.moveaxis(merged, 0, 2).reshape(rows, -1)


def cross_slab(query, keys_values):
    rows = query.shape[0]
    query = query.reshape(rows, 8, -1)
    keys_values = keys_values.reshape(rows, 2, 8, -1)
    keys, values = keys_values[:, 0], keys_values[:, 1]
    split = 2 * HD
    parts = [keys[..., :split], values[..., :split], keys[..., split:], values[..., split:], query]
    return jnp.moveaxis(jnp.concatenate(parts, axis=-1), 1, 0)


def cross_unslab(parts):
    rows = parts.shape[1]
    parts = jnp.moveaxis(parts, 0, 1)
    keys = jnp.concatenate([parts[..., :128], parts[..., 256:320]], axis=-1)
    values = jnp.concatenate([parts[..., 128:256], parts[..., 320:384]], axis=-1)
    keys_values = jnp.concatenate([keys.reshape(rows, -1), values.reshape(rows, -1)], axis=1)
    return parts[..., 384:].reshape(rows, -1), keys_values


def model_rows(column, rows, width, more=0):
    z_count = lax.axis_size("z")
    stride = column.shape[0] // z_count
    part = 4 * rows
    moves = [
        (0, z * stride + s * part, (s * z_count + z) * part, part) for s in range(2) for z in range(z_count)
    ]
    moves += [(0, z * stride + 2 * part, width + z * more, more) for z in range(z_count) if more]
    return assemble([column], moves, width + z_count * more)


def triples_to_owners(grads, rows):
    count, width = len(grads), grads[0].shape[-1]
    parts = jnp.stack([grad.reshape(-1, 4, rows, width) for grad in grads], axis=2)
    parts = jnp.moveaxis(parts, 1, 0)
    return lax.all_to_all(parts, ("y", "c"), 0, 0, tiled=True).reshape(-1, width)


def gained(grad, weight, gain):
    return grad * gain[:, None], jnp.sum(grad * weight.astype(F32), axis=1)


def head_masks(shape):
    lane = lax.broadcasted_iota(jnp.int32, shape, 1)
    return lane < HD


def rotate(values, cos_ref, down_ref, up_ref, sign):
    ahead = pltpu.roll(values, LANES - 16, 1)
    behind = pltpu.roll(values, 16, 1)
    return values * cos_ref[...] + sign * (ahead * down_ref[...] + behind * up_ref[...])


def forward_heads(query, keys, values, valid):
    left = head_masks(query.shape)
    outs, logs = [], []
    for head in range(2):
        picked = left if head == 0 else jnp.logical_not(left)
        scores = nt(jnp.where(picked, query, jnp.zeros_like(query)), keys) * 0.125
        scores = jnp.where(valid, scores, -1e30)
        peak = jnp.max(scores, axis=-1, keepdims=True)
        expo = jnp.exp(scores - peak)
        total = jnp.sum(expo, axis=-1, keepdims=True)
        probs = (expo * (1.0 / total)).astype(BF)
        outs.append(nn(probs, values))
        logs.append(peak + jnp.log(total))
    return (
        jnp.where(left, outs[0], outs[1]).astype(BF),
        jnp.where(left, logs[0], logs[1]),
    )


def backward_heads(query, keys, values, valid, logsum, grad):
    left = head_masks(query.shape)
    left_keys = head_masks(keys.shape)
    grad_q, grad_k, grad_v = [], [], []
    for head in range(2):
        picked = left if head == 0 else jnp.logical_not(left)
        none = jnp.zeros_like(query)
        scores = nt(jnp.where(picked, query, none), keys) * 0.125
        scores = jnp.where(valid, scores, -1e30)
        probs = jnp.exp(scores - logsum[:, head * HD : head * HD + 1])
        grad_probs = nt(jnp.where(picked, grad, none), values)
        delta = jnp.sum(probs * grad_probs, axis=-1, keepdims=True)
        grad_scores = (probs * (grad_probs - delta)).astype(BF)
        grad_q.append(nn(grad_scores, keys))
        grad_k.append(tn(grad_scores, query))
        grad_v.append(tn(probs.astype(BF), grad))
    return (
        jnp.where(left, grad_q[0], grad_q[1]) * 0.125,
        jnp.where(left_keys, grad_k[0], grad_k[1]) * 0.125,
        jnp.where(left_keys, grad_v[0], grad_v[1]),
    )


def one_head(query, keys, values, valid):
    scores = jnp.where(valid, nt(query, keys) * 0.125, -1e30)
    peak = jnp.max(scores, axis=-1, keepdims=True)
    expo = jnp.exp(scores - peak)
    total = jnp.sum(expo, axis=-1, keepdims=True)
    return nn((expo * (1.0 / total)).astype(BF), values), peak + jnp.log(total)


def one_head_back(query, keys, values, valid, logsum, grad):
    scores = jnp.where(valid, nt(query, keys) * 0.125, -1e30)
    probs = jnp.exp(scores - logsum)
    grad_probs = nt(grad, values)
    delta = jnp.sum(probs * grad_probs, axis=-1, keepdims=True)
    return (probs * (grad_probs - delta)).astype(BF), probs.astype(BF)


def one_head(query, keys, values, valid):
    scores = jnp.where(valid, nt(query, keys) * 0.125, -1e30)
    peak = jnp.max(scores, axis=-1, keepdims=True)
    expo = jnp.exp(scores - peak)
    total = jnp.sum(expo, axis=-1, keepdims=True)
    return nn((expo * (1.0 / total)).astype(BF), values), peak + jnp.log(total)


def one_head_back(query, keys, values, valid, logsum, grad):
    scores = jnp.where(valid, nt(query, keys) * 0.125, -1e30)
    probs = jnp.exp(scores - logsum)
    grad_probs = nt(grad, values)
    delta = jnp.sum(probs * grad_probs, axis=-1, keepdims=True)
    return (probs * (grad_probs - delta)).astype(BF), probs.astype(BF)


def self_forward_kernel(
    lengths, position, cosine, down, up, rows, weight, rotated, mixed, logsum
):
    projected = nn(rows[...], weight[...])
    pieces = [rotate(projected[:, i : i + LANES], cosine, down, up, 1.0).astype(BF) for i in (0, 128, 384)]
    values = projected[:, 256:384].astype(BF)
    values_last = projected[:, 512:576].astype(BF)
    rotated[:, 0:128] = pieces[0]
    rotated[:, 128:256] = pieces[1]
    rotated[:, 256:384] = values
    rotated[:, 384:512] = pieces[2]
    rotated[:, 512:576] = values_last
    valid = position[0:1, :] < lengths[pl.program_id(0)]
    mixed_pair, logsum_pair = forward_heads(pieces[0], pieces[1], values, valid)
    mixed[:, 0:128] = mixed_pair
    logsum[:, 0:128] = logsum_pair
    last = pieces[2]
    left = head_masks(last.shape)
    mixed_last, logsum_last = one_head(
        jnp.where(left, last, jnp.zeros_like(last)), pltpu.roll(last, HD, 1), values_last, valid
    )
    mixed[:, 128:192] = mixed_last.astype(BF)
    logsum[:, 128:192] = jnp.broadcast_to(logsum_last, mixed_last.shape)


def self_backward_kernel(
    lengths, position, cosine, down, up, rotated, logsum, grad_rows, weight, out_weight, grad_out, *partial
):
    grad = nt(grad_rows[...], out_weight[...]).astype(BF)
    valid = position[0:1, :] < lengths[pl.program_id(0)]
    back_q, back_k, back_v = backward_heads(
        rotated[:, 0:128], rotated[:, 128:256], rotated[:, 256:384], valid, logsum[:, 0:128], grad[:, 0:128]
    )
    grad_out[:, 0:128] = rotate(back_q, cosine, down, up, -1.0).astype(BF)
    grad_out[:, 128:256] = rotate(back_k, cosine, down, up, -1.0).astype(BF)
    grad_out[:, 256:384] = back_v.astype(BF)
    last = rotated[:, 384:512]
    turned = pltpu.roll(last, HD, 1)
    left = head_masks(last.shape)
    grad_last = grad[:, 128:192]
    grad_scores, probs = one_head_back(
        jnp.where(left, last, jnp.zeros_like(last)),
        turned,
        rotated[:, 512:576],
        valid,
        logsum[:, 128:129],
        grad_last,
    )
    both = jnp.where(left, nn(grad_scores, turned), pltpu.roll(tn(grad_scores, last), HD, 1)) * 0.125
    grad_out[:, 384:512] = rotate(both, cosine, down, up, -1.0).astype(BF)
    grad_out[:, 512:576] = tn(probs, grad_last).astype(BF)
    for out in partial:
        out[...] = nt(grad_out[...], weight[...]).astype(BF)


def cross_forward_kernel(
    lengths, position, rows, keys_values, weight, query, mixed, logsum
):
    query[...] = nn(rows[...], weight[...]).astype(BF)
    valid = position[0:1, :] < lengths[pl.program_id(0)]
    mixed_pair, logsum_pair = forward_heads(
        query[:, 0:128], keys_values[:, 0:128], keys_values[:, 128:256], valid
    )
    mixed[:, 0:128] = mixed_pair
    logsum[:, 0:128] = logsum_pair
    last = keys_values[:, 256:384]
    values = pltpu.roll(last, HD, 1)[:, 0:HD]
    mixed_last, logsum_last = one_head(query[:, 128:192], last[:, 0:HD], values, valid)
    mixed[:, 128:192] = mixed_last.astype(BF)
    logsum[:, 128:192] = jnp.broadcast_to(logsum_last, mixed_last.shape)


def cross_backward_kernel(
    lengths, position, query, keys_values, logsum, grad_rows, weight, out_weight, grad_q, grad_kv, *partial
):
    grad = nt(grad_rows[...], out_weight[...]).astype(BF)
    valid = position[0:1, :] < lengths[pl.program_id(0)]
    back_q, back_k, back_v = backward_heads(
        query[:, 0:128], keys_values[:, 0:128], keys_values[:, 128:256], valid, logsum[:, 0:128], grad[:, 0:128]
    )
    grad_q[:, 0:128] = back_q.astype(BF)
    grad_kv[:, 0:128] = back_k.astype(BF)
    grad_kv[:, 128:256] = back_v.astype(BF)
    last = keys_values[:, 256:384]
    keys = last[:, 0:HD]
    query_last, grad_last = query[:, 128:192], grad[:, 128:192]
    grad_scores, probs = one_head_back(
        query_last, keys, pltpu.roll(last, HD, 1)[:, 0:HD], valid, logsum[:, 128:129], grad_last
    )
    grad_q[:, 128:192] = (nn(grad_scores, keys) * 0.125).astype(BF)
    grad_kv[:, 256:384] = jnp.concatenate(
        [tn(grad_scores, query_last) * 0.125, tn(probs, grad_last)], axis=1
    ).astype(BF)
    for out in partial:
        out[...] = nt(grad_q[...], weight[...]).astype(BF)


def attention_call(kernel, lengths, tables, inputs, weights, outputs, name, micros=0):
    sequences = lengths.shape[0]

    def block(rows, width):
        return pl.BlockSpec((rows // sequences, width), lambda b, ln: (b, 0))

    def table(value):
        return pl.BlockSpec((None,) + value.shape[1:], lambda b, ln: (b, 0, 0))

    def whole(value):
        return pl.BlockSpec(value.shape, lambda b, ln: (0, 0))

    return pl.pallas_call(
        kernel,
        out_shape=[jax.ShapeDtypeStruct((r, w), dt) for r, w, dt in outputs],
        grid_spec=pltpu.PrefetchScalarGridSpec(
            num_scalar_prefetch=1,
            grid=(sequences,),
            in_specs=[table(t) for t in tables]
            + [block(*i.shape) for i in inputs]
            + [whole(w) for w in weights],
            out_specs=[block(r, w) for r, w, _ in outputs],
        ),
        compiler_params=pltpu.CompilerParams(
            dimension_semantics=("arbitrary",), vmem_limit_bytes=48 << 20
        ),
        cost_estimate=cost(micros),
        name=name,
    )(lengths, *tables, *inputs, *weights)


def feed_forward_kernel(rows, grad_rows, weights, hidden, grad_out, *partial):
    units, width = hidden.shape[1], rows.shape[1]
    gate = nn(rows[...], weights[:width, :units])
    upper = nn(rows[...], weights[:width, units:])
    sig = jax.nn.sigmoid(gate)
    silu = gate * sig
    hidden[...] = (silu * upper).astype(BF)
    grad_hidden = nt(grad_rows[...], weights[width:])
    grad_out[:, :units] = (grad_hidden * upper * (sig * (1.0 + gate * (1.0 - sig)))).astype(BF)
    grad_out[:, units:] = (grad_hidden * silu).astype(BF)
    for out in partial:
        out[...] = nt(grad_out[...], weights[:width]).astype(BF)


def feed_forward(rows, grad_rows, weights, partial):
    total, width = rows.shape
    units = weights.shape[1] // 2
    block = total // 2

    def whole(value):
        return pl.BlockSpec(value.shape, lambda i: (0, 0))

    widths = [units, 2 * units] + [width] * partial
    return pl.pallas_call(
        feed_forward_kernel,
        out_shape=[jax.ShapeDtypeStruct((total, w), BF) for w in widths],
        grid=(2,),
        in_specs=[pl.BlockSpec((block, width), lambda i: (i, 0))] * 2 + [whole(weights)],
        out_specs=[pl.BlockSpec((block, w), lambda i: (i, 0)) for w in widths],
        compiler_params=pltpu.CompilerParams(vmem_limit_bytes=56 << 20),
        cost_estimate=cost(10),
        name="feed_forward",
    )(rows, grad_rows, weights)


def weight_grad_kernel(here, there, grad_here, grad_there, out):
    grad = tn(here[...], grad_here[...]) + tn(there[...], grad_there[...])
    out[...] = grad.astype(BF).reshape(out.shape)


def weight_grad(rows, grads, own_rows=None):
    total, width = rows[0].shape
    columns = grads[0].shape[1]
    block = 3 * LANES
    steps = width // block
    if own_rows is None:
        out_shape, out_block = (width, columns), pl.BlockSpec((block, columns), lambda i: (i, 0))
    else:
        z_count, part = lax.axis_size("z"), 4 * own_rows
        turn = steps // 2
        out_shape = (z_count, 2, part, columns)
        out_block = pl.BlockSpec((block // part, None, part, columns), lambda i: (i % turn, i // turn, 0, 0))
    return pl.pallas_call(
        weight_grad_kernel,
        out_shape=jax.ShapeDtypeStruct(out_shape, BF),
        grid=(steps,),
        in_specs=[pl.BlockSpec((total, block), lambda i: (0, i))] * 2
        + [pl.BlockSpec((total, columns), lambda i: (0, 0))] * 2,
        out_specs=out_block,
        compiler_params=pltpu.CompilerParams(vmem_limit_bytes=48 << 20),
        cost_estimate=cost(total * width * columns / 2e8),
        name="weight_grad",
    )(*rows, *grads)


def spread_gate_kernel(unit, gain, weight, out):
    scaled = weight[...].astype(F32) * gain[...]
    corners, _, width = out.shape
    for z in range(width // unit):
        for corner in range(corners):
            start = (z * corners + corner) * unit
            out[corner, :, z * unit : (z + 1) * unit] = scaled[:, start : start + unit].astype(BF)


def spread_gate(weight, gain, unit):
    rows, columns = weight.shape
    quarter = columns // 4
    return pl.pallas_call(
        functools.partial(spread_gate_kernel, unit),
        out_shape=jax.ShapeDtypeStruct((8, rows, columns // 8), BF),
        grid=(2, 2),
        in_specs=[
            pl.BlockSpec((rows, 1), lambda g, s: (0, 0)),
            pl.BlockSpec((rows, quarter), lambda g, s: (0, 2 * g + s)),
        ],
        out_specs=pl.BlockSpec((4, rows, quarter // 4), lambda g, s: (s, 0, g)),
        cost_estimate=cost(0),
        name="spread_gate",
    )(gain[:, None], weight)


def collect_gate_kernel(unit, gain, weight, grads, out, sums):
    @pl.when((pl.program_id(0) == 0) & (pl.program_id(1) == 0))
    def _():
        sums[...] = jnp.zeros_like(sums)

    corners, rows, width = grads.shape
    total = jnp.zeros((rows, 2 * unit), F32)
    for z in range(width // unit):
        for corner in range(0, corners, 2):
            cut = slice((z * corners + corner) * unit, (z * corners + corner + 2) * unit)
            pair = [grads[corner + i, :, z * unit : (z + 1) * unit] for i in range(2)]
            grad = jnp.concatenate(pair, axis=1).astype(F32)
            out[:, cut] = grad * gain[...]
            total = total + grad * weight[:, cut].astype(F32)
    sums[...] = sums[...] + jnp.sum(total, axis=1, keepdims=True)


def collect_gate(grads, weight, gain, unit):
    rows, columns = weight.shape
    quarter = columns // 4
    grad, sums = pl.pallas_call(
        functools.partial(collect_gate_kernel, unit),
        out_shape=[jax.ShapeDtypeStruct((rows, columns), F32), jax.ShapeDtypeStruct((rows, LANES), F32)],
        grid=(2, 2),
        in_specs=[
            pl.BlockSpec((rows, 1), lambda g, s: (0, 0)),
            pl.BlockSpec((rows, quarter), lambda g, s: (0, 2 * g + s)),
            pl.BlockSpec((4, rows, quarter // 4), lambda g, s: (s, 0, g)),
        ],
        out_specs=[
            pl.BlockSpec((rows, quarter), lambda g, s: (0, 2 * g + s)),
            pl.BlockSpec((rows, LANES), lambda g, s: (0, 0)),
        ],
        cost_estimate=cost(10),
        name="collect_gate",
    )(gain[:, None], weight, grads)
    return grad, sums[:, 0]


def normalize(hidden):
    centred = hidden - jnp.mean(hidden, axis=-1, keepdims=True)
    inverse = lax.rsqrt(jnp.mean(centred * centred, axis=-1, keepdims=True) + 1e-05)
    return centred * inverse, inverse


def layer_norm_back(hidden, scaled):
    unit, inverse = normalize(hidden)
    return inverse * (
        scaled
        - jnp.mean(scaled, axis=-1, keepdims=True)
        - unit * jnp.mean(scaled * unit, axis=-1, keepdims=True)
    )


def total_of(parts):
    return parts[0][...] + parts[1][...].astype(F32) + parts[2][...].astype(F32)


def lane_sums(value):
    sums = jnp.sum(value, axis=0, keepdims=True)
    return sum(sums[:, i : i + LANES] for i in range(0, sums.shape[1], LANES))


def forward_rows_kernel(bounds, stream, *refs):
    parts, (stream_out, low_out, high_out, squares) = (refs[:3], refs[3:6]), refs[6:]
    half = low_out.shape[0]
    sums = [0.0, 0.0]
    for index, out in enumerate((low_out, high_out)):
        rows = slice(index * half, (index + 1) * half)
        branch = total_of(parts[index])
        hidden = stream[rows] + branch
        stream_out[rows] = hidden
        out[...] = normalize(hidden)[0].astype(BF)
        position = bounds[0] + index * half + lax.broadcasted_iota(jnp.int32, (half, 1), 0)
        weight = jnp.where(position < bounds[1], 1.0, 0.0)
        sums = [sums[0] + lane_sums(branch * branch * weight), sums[1] + lane_sums(hidden * hidden * weight)]
    squares[0:1] = sums[0]
    squares[1:2] = sums[1]


def last_rows_kernel(bounds, stream, *refs):
    parts, (stream_out, squares) = (refs[:3], refs[3:6]), refs[6:]
    half = parts[0][0].shape[0]
    sums = [0.0, 0.0]
    for index in range(2):
        rows = slice(index * half, (index + 1) * half)
        branch = total_of(parts[index])
        hidden = stream[rows] + branch
        stream_out[rows] = hidden.astype(BF)
        position = bounds[0] + index * half + lax.broadcasted_iota(jnp.int32, (half, 1), 0)
        weight = jnp.where(position < bounds[1], 1.0, 0.0)
        sums = [sums[0] + lane_sums(branch * branch * weight), sums[1] + lane_sums(hidden * hidden * weight)]
    squares[0:1] = sums[0]
    squares[1:2] = sums[1]


def backward_rows_kernel(grad, stream, *refs):
    parts, outs = (refs[:3], refs[3:6]), refs[6:]
    half = parts[0][0].shape[0]
    for index in range(2):
        rows = slice(index * half, (index + 1) * half)
        total = grad[rows].astype(F32) + layer_norm_back(stream[rows].astype(F32), total_of(parts[index]))
        outs[0][rows] = total
        if len(outs) > 1:
            outs[1 + index][...] = total.astype(BF)


def rows_call(kernel, leading, parts, outputs, name, micros=0):
    vmem = pl.BlockSpec(memory_space=pltpu.VMEM)
    smem = pl.BlockSpec(memory_space=pltpu.SMEM)
    operands = list(leading) + list(parts[0]) + list(parts[1])
    return pl.pallas_call(
        kernel,
        out_shape=[jax.ShapeDtypeStruct(shape, dt) for shape, dt in outputs],
        in_specs=[smem if o.ndim == 1 else vmem for o in operands],
        out_specs=[vmem] * len(outputs),
        compiler_params=pltpu.CompilerParams(vmem_limit_bytes=48 << 20),
        cost_estimate=cost(micros),
        name=name,
    )(*operands)


def shards(
    tokens,
    conditioning,
    seq_lengths,
    cond_lengths,
    norm_gains,
    w_qkv,
    w_self_out,
    w_cross_q,
    w_cross_kv,
    w_cross_out,
    w_gate_up,
    w_down,
    out_grad,
):
    rows, width = tokens.shape
    half = rows // 2
    z_count = lax.axis_size("z")
    own_rows = w_qkv.shape[0]
    hidden_own = w_down.shape[0]
    s_rank, z_rank = lax.axis_index("s"), lax.axis_index("z")
    y_rank, c_rank = lax.axis_index("y"), lax.axis_index("c")
    span = 2 * rows

    first_seq = (z_rank * 2 + y_rank) * 2
    mine, other = first_seq + c_rank, first_seq + 1 - c_rank
    across, corner = (z_rank * 2 + 1 - y_rank) * 2 + c_rank, (z_rank * 2 + 1 - y_rank) * 2 + 1 - c_rank
    seq_here = jnp.stack([seq_lengths[mine], seq_lengths[across]])
    seq_there = jnp.stack([seq_lengths[other], seq_lengths[corner]])
    cond_here_lengths = jnp.stack([cond_lengths[mine], cond_lengths[across]])
    cond_there_lengths = jnp.stack([cond_lengths[other], cond_lengths[corner]])
    bounds = jnp.stack([s_rank * rows, seq_lengths[mine]])
    positions = half_positions(s_rank, rows)
    lane = jnp.arange(LANES, dtype=jnp.int32) % HD
    freqs = jnp.exp((lane % 16).astype(F32) * (-math.log(10000.0) / 16.0))
    angles = positions.astype(F32)[..., None] * freqs
    cosine = jnp.where(lane < 32, jnp.cos(angles), 1.0)
    sine = jnp.sin(angles)
    down = jnp.where(lane < 16, -sine, 0.0)
    up = jnp.where((lane >= 16) & (lane < 32), sine, 0.0)
    tables = [jnp.broadcast_to(positions[:, None, :], (2, 8, span)), cosine, down, up]
    cond_rows = conditioning.shape[0]
    cond_position = jnp.broadcast_to(jnp.arange(cond_rows, dtype=jnp.int32), (2, 8, cond_rows))

    eight = ("s", "y", "c")
    gains = norm_gains.astype(F32)
    qkv_parts = slab((w_qkv.astype(F32) * gains[0][:, None]).astype(BF))
    qkv_parts = lax.all_to_all(qkv_parts, eight, 0, 0, tiled=True)
    slab_width = qkv_parts.shape[-1]
    head_width = slab_width // 3
    slab_rows = 8 * own_rows

    def out_rows(column):
        column = column.reshape(z_count, -1, slab_width)[:, slab_rows:].reshape(4, -1, own_rows, width)
        column = lax.all_to_all(column, ("y", "c"), 0, 0, tiled=True)
        return jnp.moveaxis(column, 0, 1).reshape(-1, width)

    qkv_both = jnp.concatenate([qkv_parts.reshape(slab_rows, -1), w_self_out.reshape(-1, slab_width)], axis=0)
    qkv_column = gather_z(qkv_both)
    first_unit = normalize(tokens.astype(F32))[0].astype(BF)
    first, arrived = gather_eight(first_unit[:half], first_unit[half:])
    conditioning, cross_q_own, cross_kv_own = after((conditioning, w_cross_q, w_cross_kv), (first[0], qkv_both))
    cond_here = jnp.concatenate([conditioning, swap(conditioning, "y")], axis=0)
    cond = (cond_here, swap(cond_here, "c"))
    cross_parts = cross_slab((cross_q_own.astype(F32) * gains[1][:, None]).astype(BF), cross_kv_own)
    cross_parts = lax.all_to_all(cross_parts, eight, 0, 0, tiled=True)
    cross_both = jnp.concatenate([cross_parts.reshape(slab_rows, -1), w_cross_out.reshape(-1, slab_width)], axis=0)
    cross_column = gather_z(cross_both)
    gate_parts = spread_gate(after(w_gate_up, first[0]), gains[2], hidden_own)
    gate_parts = lax.all_to_all(after(gate_parts, (cross_both, cond_here)), eight, 0, 0, tiled=True)
    qkv_column = after(qkv_column, cond_here)
    qkv_full = model_rows(qkv_column, own_rows, width)

    def self_attention(side, lengths):
        return attention_call(
            self_forward_kernel,
            lengths,
            tables,
            [first[side]],
            [qkv_full],
            [(2 * span, slab_width, BF), (2 * span, head_width, BF), (2 * span, head_width, F32)],
            "self_forward",
            7,
        )

    out_grads_all, arrived = gather_eight(*after((out_grad[:half], out_grad[half:]), qkv_full))
    self_here = self_attention(0, seq_here)
    self_out_full = out_rows(after(qkv_column, self_here[1]))
    self_there = self_attention(1, seq_there)
    ff_column = gather_z(
        jnp.concatenate([after(gate_parts, self_here[1]).reshape(slab_rows, -1), w_down], axis=0)
    )
    (self_partial,) = project(after(self_there[1], (arrived, out_grads_all[0])), self_out_full, nn, width)
    parts, sent = reduce_eight(project(self_here[1], self_out_full, nn, width, swap(self_partial, "c")))
    forward_outs = [((rows, width), F32), ((half, width), BF), ((half, width), BF), ((8, LANES), F32)]
    cross_column = after(cross_column, sent)
    cross_full = model_rows(cross_column, own_rows, width)
    kv_width = 2 * head_width
    cross_kv_full, cross_q_full = cross_full[:, :kv_width], cross_full[:, kv_width:]
    cond_proj = [nn(c, cross_kv_full).astype(BF) for c in cond]
    parts = after(parts, (cond_proj, cross_q_full))
    after_self, second_low, second_high, squares_self = rows_call(
        forward_rows_kernel, [bounds, tokens.astype(F32)], parts, forward_outs, "forward_rows"
    )

    second, arrived = gather_eight(second_low, second_high)
    cross_out_full = out_rows(after(cross_column, arrived))

    def cross_attention(side, lengths):
        return attention_call(
            cross_forward_kernel,
            lengths,
            [cond_position],
            [second[side], cond_proj[side]],
            [cross_q_full],
            [(2 * span, head_width, BF), (2 * span, head_width, BF), (2 * span, head_width, F32)],
            "cross_forward",
        )

    cross_here = cross_attention(0, cond_here_lengths)
    cross_there = cross_attention(1, cond_there_lengths)
    (cross_partial,) = project(cross_there[1], cross_out_full, nn, width)
    parts, sent = reduce_eight(project(cross_here[1], cross_out_full, nn, width, swap(cross_partial, "c")))
    ff_full = model_rows(after(ff_column, sent), own_rows, width, hidden_own)
    parts = after(parts, ff_full)
    after_cross, third_low, third_high, squares_cross = rows_call(
        forward_rows_kernel, [bounds, after_self], parts, forward_outs, "forward_rows"
    )

    third, _ = gather_eight(third_low, third_high)
    hidden_there, gates_there, back_there = feed_forward(third[1], out_grads_all[1], ff_full, 1)
    hidden_here, gates_here = feed_forward(third[0], out_grads_all[0], ff_full, 0)
    blocks = project(gates_here, ff_full, nt, width, swap(back_there, "c"), micros=8)
    down_grad = weight_grad(after((hidden_here, hidden_there), blocks), out_grads_all)
    d_down = scatter_z(down_grad)
    parts, sent = reduce_eight(blocks, 2, down_grad)
    backward_outs = [((rows, width), F32), ((half, width), BF), ((half, width), BF)]
    grad_after_cross, cross_low, cross_high = rows_call(
        backward_rows_kernel, [out_grad, after_cross], parts, backward_outs, "backward_rows", 3
    )

    cross_grad, gate_grad = gather_eight(
        cross_low,
        cross_high,
        3,
        lambda arrived: weight_grad(third, after((gates_here, gates_there), arrived), own_rows),
    )
    gate_grads = scatter_z(after(gate_grad, d_down).reshape(-1, gate_grad.shape[-1]))

    def cross_attention_back(side, forward, lengths, partial):
        return attention_call(
            cross_backward_kernel,
            lengths,
            [cond_position],
            [forward[0], cond_proj[side], forward[2], cross_grad[side]],
            [cross_q_full, cross_out_full],
            [(2 * span, head_width, BF), (2 * cond_rows, kv_width, BF)] + [(2 * span, width, BF)] * partial,
            "cross_backward",
            5,
        )

    back_there = cross_attention_back(1, cross_there, cond_there_lengths, 1)
    back_here = cross_attention_back(0, cross_here, cond_here_lengths, 0)
    parts, sent = reduce_eight(
        project(back_here[0], cross_q_full, nt, width, swap(back_there[2], "c"), micros=5), 2
    )
    back_queries, back_keys = after(((back_here[0], back_there[0]), (back_here[1], back_there[1])), sent)
    cross_grads = jnp.concatenate(
        [weight_grad(cond, back_keys, own_rows), weight_grad(second, back_queries, own_rows)], axis=-1
    )
    cross_out_grad = (tn(cross_here[1], cross_grad[0]) + tn(cross_there[1], cross_grad[1])).astype(BF)
    parts = after(parts, (cross_grads, cross_out_grad, d_down))
    grad_after_self, self_low, self_high = rows_call(
        backward_rows_kernel, [grad_after_cross, after_self], parts, backward_outs, "backward_rows", 3
    )

    self_grad, sent = gather_eight(self_low, self_high, 3)
    down_block = width // hidden_here.shape[1]
    (mlp_there,) = project(after(hidden_there, sent), ff_full, nn, width, None, down_block, 5)
    mlp_there = swap(mlp_there, "c")
    cross_grads = scatter_z(after(cross_grads, (gate_grads, self_grad[0])).reshape(-1, slab_width))

    def self_attention_back(side, forward, lengths, partial):
        return attention_call(
            self_backward_kernel,
            lengths,
            tables,
            [forward[0], forward[2], self_grad[side]],
            [qkv_full, self_out_full],
            [(2 * span, slab_width, BF)] + [(2 * span, width, BF)] * partial,
            "self_backward",
            10,
        )

    proj_there, back_there = self_attention_back(1, self_there, seq_there, 1)
    earlier = after((self_grad, back_keys), proj_there)
    self_out_grad = (tn(self_here[1], earlier[0][0]) + tn(self_there[1], earlier[0][1])).astype(BF)
    out_grads = triples_to_owners((self_out_grad, cross_out_grad), own_rows)
    cond_there = swap(nt(earlier[1][1], cross_kv_full).astype(BF), "c")
    self_grad = (after(self_grad[0], self_out_grad), self_grad[1])
    (proj_here,) = self_attention_back(0, self_here, seq_here, 0)
    cond_back = nt(earlier[1][0], cross_kv_full) + after(cond_there, proj_here).astype(F32)
    cond_across = swap(cond_back[cond_rows:].astype(BF), "y")
    gate_grads = lax.all_to_all(after(gate_grads, proj_here).reshape(8, own_rows, -1), eight, 0, 0, tiled=True)
    proj_here = after(proj_here, cross_grads)
    out_grads = scatter_z(after(out_grads, cross_grads))
    qkv_grads = weight_grad(first, (proj_here, proj_there), own_rows)
    blocks = project(after(proj_here, out_grads), qkv_full, nt, width, swap(back_there, "c"), micros=5)
    parts, sent = reduce_eight(blocks, 2)
    mlp_blocks = project(after(hidden_here, qkv_grads), ff_full, nn, width, mlp_there, down_block, 5)
    qkv_grads = scatter_z(after(qkv_grads, out_grads).reshape(-1, slab_width))
    mlp_parts, mlp_sent = reduce_eight(mlp_blocks, 2)
    cond_back = cond_back[:cond_rows] + after(cond_across, mlp_blocks).astype(F32)
    d_conditioning = cond_back.astype(BF).astype(F32) + swap(cond_back.astype(BF), "s").astype(F32)
    (d_tokens,) = rows_call(
        backward_rows_kernel, [grad_after_self, tokens], parts, backward_outs[:1], "backward_rows", 3
    )
    block_out, squares_last = rows_call(
        last_rows_kernel,
        [bounds, after_cross],
        mlp_parts,
        [((rows, width), BF), ((8, LANES), F32)],
        "last_rows",
        3,
    )
    squares = jnp.concatenate([squares_self[:2], squares_cross[:2], squares_last[:2], squares_last[:2]], axis=0)
    squares = sum_everywhere(after(squares, blocks))
    qkv_grads = after(qkv_grads, squares).reshape(8, own_rows, -1)
    qkv_parts = lax.all_to_all(qkv_grads, eight, 0, 0, tiled=True)
    squares = jnp.sum(squares, axis=1)[:6]
    rms_stats = jnp.sqrt(squares / (jnp.sum(seq_lengths).astype(F32) * width))

    d_down = after(d_down, proj_here).astype(F32)
    gate_grads = after(gate_grads, (squares_last, blocks))
    d_gate_up, gain_third = collect_gate(gate_grads, w_gate_up, gains[2], hidden_own)
    cross_grads = lax.all_to_all(cross_grads.reshape(8, own_rows, -1), eight, 0, 0, tiled=True)
    d_cross_q, d_cross_kv = cross_unslab(cross_grads)
    d_cross_q, gain_second = gained(d_cross_q.astype(F32), w_cross_q, gains[1])
    d_qkv, gain_first = gained(unslab(qkv_parts).astype(F32), w_qkv, gains[0])
    return (
        block_out,
        d_tokens,
        d_conditioning,
        jnp.stack([gain_first, gain_second, gain_third]),
        d_qkv,
        out_grads[:own_rows].astype(F32),
        d_cross_q,
        d_cross_kv.astype(F32),
        out_grads[own_rows:].astype(F32),
        d_gate_up,
        d_down,
        rms_stats,
    )


def solution(mesh):
    seq_count, fsdp_count = mesh.devices.shape
    fine = Mesh(mesh.devices.reshape(seq_count, fsdp_count // 4, 2, 2), ALL)
    by_token = P(("z", "y", "c", "s"), None)
    by_sequence = P(("z", "y", "c"), None)
    by_row = P(ALL, None)
    by_column = P(None, ALL)
    return jax.shard_map(
        shards,
        mesh=fine,
        in_specs=(by_token, by_sequence, P(), P(), by_column) + (by_row,) * 7 + (by_token,),
        out_specs=(by_token, by_token, by_sequence, by_column) + (by_row,) * 7 + (P(),),
        check_vma=False,
    )
```
